32 devices in a mesh: seq: 16 (over z, y, x), chan: 2 (over core).
Axes of the slice: x: 2, y: 2, z: 4, core: 2. Of those that a mesh axis runs over, the one named last changes fastest.
Arguments:
- inputs: float32 [256, 8192], P('chan', 'seq'), may hold values from -6 to 6
- value_weight: float32 [256, 256], P(None, 'chan'), may hold values from -0.375 to 0.375
- query_weight: float32 [256, 256], P(None, 'chan'), may hold values from -0.375 to 0.375
- filters: float32 [256, 8192], P('chan', 'seq'), may hold values from -1 to 1
- grad_out: float32 [256, 8192], P('chan', 'seq'), may hold values from -6 to 6
Outputs:
- input_grad: float32 [256, 8192], P('chan', 'seq')
- filter_grad: float32 [256, 8192], P('chan', 'seq')
- value_gradient: float32 [256, 256], P(None, 'chan')
- query_gradient: float32 [256, 256], P(None, 'chan')
The draws below stay inside these ranges and needn't reach their ends.
All inputs are finite; a program needn't handle non-finite values.
Results may differ from the reference program's by a relative error of at most 0.00018.
Values sent between devices are 32-bit elements; how exact they have to be, the bound alone decides.
A program may use at most 64 MiB of HBM per device.

```python
import math
import jax
import jax.numpy as jnp
from jax import lax

C = 256
SEQ = 8192


def draw_filters(key, part):
    rate_key = jax.random.fold_in(key, 11)
    noise_key = jax.random.fold_in(key, 12)
    log_rate = jax.random.uniform(rate_key, (C, 1), jnp.float32, math.log(0.5 / SEQ), math.log(1.0 / 40.0))
    noise = jnp.clip(jax.random.normal(noise_key, (C, SEQ), jnp.float32), -4.0, 4.0)
    decay_rate = jnp.exp(log_rate)
    lag_values = jnp.arange(SEQ, dtype=jnp.float32)[None, :]
    energy = jnp.expm1(-2.0 * decay_rate * SEQ) / jnp.expm1(-2.0 * decay_rate)
    return noise * jnp.exp(-decay_rate * lag_values) / jnp.sqrt(energy)


def steps_of(own_key, extent, cuts, least, high):
    factor_of, own = 1.0, jax.random.fold_in(own_key, 6)
    for axis_at, parts in cuts:
        steps = jnp.exp(jax.random.uniform(jax.random.fold_in(own, axis_at), (parts,), jnp.float32, least / len(cuts), high / len(cuts)))
        factor_of = factor_of * jnp.repeat(steps, extent[axis_at] // parts).reshape([-1 if axis == axis_at else 1 for axis in range(len(extent))])
    return factor_of


def centred(stream_key, shape, width, reach, pieces=(), kind=jnp.bfloat16):
    level = steps_of(stream_key, shape, pieces, -0.22, 0.18) if pieces else 1.0
    array = jax.random.normal(stream_key, shape, jnp.float32) * width * level
    return jnp.minimum(jnp.maximum(array, -reach), reach).astype(kind)


def setup_inputs(seed: int = 0) -> dict:
    key_of = jax.random.split(jax.random.key(seed), 6)
    inputs = centred(key_of[0], (C, SEQ), 1.0, 6.0, ((0, 2), (1, 16)), jnp.float32)
    value_weight = centred(key_of[1], (C, C), C ** -0.5, 0.375, ((1, 2),), jnp.float32)
    query_weight = centred(key_of[2], (C, C), C ** -0.5, 0.375, ((1, 2),), jnp.float32)
    filters = draw_filters(jax.random.fold_in(key_of[5], 71), 0)
    grad_out = centred(key_of[4], (C, SEQ), 1.0, 6.0, ((0, 2), (1, 16)), jnp.float32)
    return dict(inputs=inputs, value_weight=value_weight, query_weight=query_weight, filters=filters, grad_out=grad_out)


def correlate(blocks):
    projected, filters, gated_grad = blocks
    seq_length = projected.shape[1]
    padded = 2 * seq_length
    value_spec = jnp.fft.rfft(projected, n=padded, axis=1)
    filter_spec = jnp.fft.rfft(filters, n=padded, axis=1)
    grad_spec = jnp.fft.rfft(gated_grad, n=padded, axis=1)
    convolved = jnp.fft.irfft(filter_spec * value_spec, n=padded, axis=1)[:, :seq_length]
    grad_value = jnp.fft.irfft(jnp.conj(filter_spec) * grad_spec, n=padded, axis=1)[:, :seq_length]
    filter_grad = jnp.fft.irfft(jnp.conj(value_spec) * grad_spec, n=padded, axis=1)[:, :seq_length]
    return jnp.stack([convolved, grad_value, filter_grad])


def reference(inputs, value_weight, query_weight, filters, grad_out):
    precise = lax.Precision.HIGHEST
    channel_count = inputs.shape[0]
    seq_length = inputs.shape[1]
    grad_scale = seq_length ** -0.5
    projected = jnp.dot(value_weight.T, inputs, precision=precise, preferred_element_type=jnp.float32)
    query_proj = jnp.dot(query_weight.T, inputs, precision=precise, preferred_element_type=jnp.float32)
    gated_grad = grad_out * query_proj
    group_count = channel_count // 16
    results = lax.map(correlate, (projected.reshape(group_count, 16, seq_length), filters.reshape(group_count, 16, seq_length), gated_grad.reshape(group_count, 16, seq_length)))
    convolved = results[:, 0].reshape(channel_count, seq_length)
    grad_value = results[:, 1].reshape(channel_count, seq_length)
    filter_grad = results[:, 2].reshape(channel_count, seq_length) * grad_scale
    grad_query = grad_out * convolved
    input_grad = jnp.dot(value_weight, grad_value, precision=precise, preferred_element_type=jnp.float32) + jnp.dot(query_weight, grad_query, precision=precise, preferred_element_type=jnp.float32)
    value_gradient = jnp.dot(inputs, grad_value.T, precision=precise, preferred_element_type=jnp.float32) * grad_scale
    query_gradient = jnp.dot(inputs, grad_query.T, precision=precise, preferred_element_type=jnp.float32) * grad_scale
    return (input_grad, filter_grad, value_gradient, query_gradient)
```

```python
import functools
import math

import jax
import jax.numpy as jnp
import numpy as np
from jax import lax
from jax.experimental import pallas as pl
from jax.experimental.pallas import tpu as pltpu
from jax.sharding import PartitionSpec as P

BLK = 64
LANES = 128
GROUP = 8


HIGHEST = lax.Precision.HIGHEST


def complex_table(row_count, col_count, period, direction):
    row_iota = lax.broadcasted_iota(jnp.int32, (row_count, col_count), 0)
    col_iota = lax.broadcasted_iota(jnp.int32, (row_count, col_count), 1)
    rotation = 2.0 * math.pi / period * (row_iota * col_iota % period).astype(jnp.float32)
    cosine = jnp.cos(rotation)
    sine_part = direction * jnp.sin(rotation)
    upper_rows = jnp.stack([cosine, sine_part], axis=1)
    lower_rows = jnp.stack([-sine_part, cosine], axis=1)
    return jnp.stack([upper_rows, lower_rows], axis=0)


def rotate(columns, cosine, sine_part):
    return jnp.stack(
        [columns[0] * cosine - columns[1] * sine_part, columns[0] * sine_part + columns[1] * cosine]
    )


def multiply(first_spec, second_spec, conjugate):
    imag_first = -first_spec[1] if conjugate else first_spec[1]
    return jnp.stack(
        [
            first_spec[0] * second_spec[0] - imag_first * second_spec[1],
            first_spec[0] * second_spec[1] + imag_first * second_spec[0],
        ]
    )


def block_angles(block_size, inner_size, seq_rows, direction):
    outer_iota = lax.broadcasted_iota(jnp.int32, (block_size, inner_size), 0)
    inner_iota = lax.broadcasted_iota(jnp.int32, (block_size, inner_size), 1)
    rotation = (
        direction
        * 2.0
        * math.pi
        / seq_rows
        * (outer_iota * inner_iota % seq_rows).astype(jnp.float32)
    )
    return (jnp.cos(rotation)[:, :, None], jnp.sin(rotation)[:, :, None])


def local_forward(columns, block_size):
    seq_rows = columns.shape[1]
    item_width = columns.shape[2]
    inner_size = seq_rows // block_size
    shaped = columns.reshape(2, block_size, inner_size, item_width)
    first_pass = jnp.einsum(
        "xabz,xayk->ykbz",
        shaped,
        complex_table(block_size, block_size, block_size, -1.0),
        precision=HIGHEST,
    )
    cosine, sine_part = block_angles(block_size, inner_size, seq_rows, -1.0)
    rotated = rotate(first_pass, cosine, sine_part)
    second = jnp.einsum(
        "ykbz,ybwm->wkmz",
        rotated,
        complex_table(inner_size, inner_size, inner_size, -1.0),
        precision=HIGHEST,
    )
    return second.reshape(2, seq_rows, item_width)


def local_inverse(columns, block_size):
    seq_rows = columns.shape[1]
    item_width = columns.shape[2]
    inner_size = seq_rows // block_size
    shaped = columns.reshape(2, block_size, inner_size, item_width)
    first_pass = jnp.einsum(
        "xkmz,xmyb->ykbz",
        shaped,
        complex_table(inner_size, inner_size, inner_size, 1.0),
        precision=HIGHEST,
    )
    cosine, sine_part = block_angles(block_size, inner_size, seq_rows, 1.0)
    rotated = rotate(first_pass, cosine, sine_part)
    second = jnp.einsum(
        "xkbz,xkya->yabz",
        rotated,
        complex_table(block_size, block_size, block_size, 1.0),
        precision=HIGHEST,
    )
    return second.reshape(2, seq_rows, item_width) * (1.0 / seq_rows)


def cross_transform(columns, dft_table):
    seq_rows = columns.shape[1]
    item_width = columns.shape[2]
    shaped = columns.reshape(2, 1, seq_rows, item_width)
    transformed = jnp.einsum(
        "xpjz,xpyk->ykjz",
        lax.all_to_all(shaped, "seq", split_axis=2, concat_axis=1, tiled=True),
        dft_table,
        precision=HIGHEST,
    )
    result = lax.all_to_all(transformed, "seq", split_axis=1, concat_axis=2, tiled=True)
    return result.reshape(2, seq_rows, item_width)


def shard_twiddle(columns, frequency, seq_length, direction):
    seq_rows = columns.shape[1]
    local_pos = jnp.arange(seq_rows, dtype=jnp.int32)
    rotation = (
        direction
        * 2.0
        * math.pi
        / seq_length
        * (local_pos * frequency % seq_length).astype(jnp.float32)
    )
    return rotate(columns, jnp.cos(rotation)[:, None], jnp.sin(rotation)[:, None])


def forward(columns, shard_index, devices, block_size):
    seq_length = columns.shape[1] * devices
    columns = cross_transform(columns, complex_table(devices, devices, devices, -1.0))
    columns = shard_twiddle(columns, shard_index, seq_length, -1.0)
    return local_forward(columns, block_size)


def inverse(columns, shard_index, devices, block_size):
    seq_length = columns.shape[1] * devices
    columns = local_inverse(columns, block_size)
    columns = shard_twiddle(columns, shard_index, seq_length, 1.0)
    columns = cross_transform(
        columns, complex_table(devices, devices, devices, 1.0) * (1.0 / devices)
    )
    return columns


def per_device(inputs, value_weight, query_weight, filters, grad_out):
    channel_count = filters.shape[0]
    seq_rows = filters.shape[1]
    devices = lax.axis_size("seq")
    shard_index = lax.axis_index("seq")
    seq_length = seq_rows * devices
    grad_scale = 1.0 / math.sqrt(seq_length)
    all_inputs = lax.all_gather(inputs, "chan", axis=0, tiled=True)
    projected = jnp.einsum("cd,ct->dt", value_weight, all_inputs, precision=HIGHEST)
    query_proj = jnp.einsum("cd,ct->dt", query_weight, all_inputs, precision=HIGHEST)
    gated_grad = grad_out * query_proj
    signals = jnp.stack([projected, filters, gated_grad])
    position = shard_index * seq_rows + jnp.arange(seq_rows, dtype=jnp.int32)
    twist_angle = 0.5 * math.pi / seq_length * position.astype(jnp.float32)
    cosine = jnp.cos(twist_angle)
    sine_part = jnp.sin(twist_angle)
    twisted = jnp.stack([signals * cosine, -signals * sine_part])
    columns = jnp.transpose(twisted, (0, 3, 1, 2)).reshape(2, seq_rows, 3 * channel_count)
    spectra = forward(columns, shard_index, devices, BLK).reshape(2, seq_rows, 3, channel_count)
    value_spec = spectra[:, :, 0]
    filter_spec = spectra[:, :, 1]
    grad_spec = spectra[:, :, 2]
    products = jnp.stack(
        [
            multiply(filter_spec, value_spec, False),
            multiply(filter_spec, grad_spec, True),
            multiply(value_spec, grad_spec, True),
        ],
        axis=2,
    )
    restored = inverse(
        products.reshape(2, seq_rows, 3 * channel_count), shard_index, devices, BLK
    ).reshape(2, seq_rows, 3, channel_count)
    combined = restored[0] * cosine[:, None, None] - restored[1] * sine_part[:, None, None]
    combined = jnp.transpose(combined, (1, 2, 0))
    convolved = combined[0]
    grad_value = combined[1]
    filter_grad = combined[2] * grad_scale
    grad_query = grad_out * convolved
    input_grad = lax.psum_scatter(
        jnp.dot(value_weight, grad_value, precision=HIGHEST, preferred_element_type=jnp.float32)
        + jnp.dot(query_weight, grad_query, precision=HIGHEST, preferred_element_type=jnp.float32),
        "chan",
        scatter_dimension=0,
        tiled=True,
    )
    partial_value = jnp.einsum("ct,dt->cd", all_inputs, grad_value, precision=HIGHEST) * grad_scale
    partial_query = jnp.einsum("ct,dt->cd", all_inputs, grad_query, precision=HIGHEST) * grad_scale
    value_gradient, query_gradient = lax.psum((partial_value, partial_query), "seq")
    return (input_grad, filter_grad, value_gradient, query_gradient)


NN = (((1,), (0,)), ((), ()))
NT = (((1,), (1,)), ((), ()))


def split_table(table):
    high = table.astype(jnp.bfloat16)
    low = (table - high.astype(np.float32)).astype(jnp.bfloat16)
    return high, low


@functools.lru_cache(maxsize=None)
def transform_tables(seq_length):
    outer = seq_length // LANES
    k = np.arange(outer, dtype=np.float64)
    a = np.arange(outer, dtype=np.float64)
    b = np.arange(LANES, dtype=np.float64)
    phase = 2 * np.pi * np.outer(4 * k + 1, a) % (2 * np.pi * 4 * outer) / (4 * outer)
    small = np.concatenate([np.cos(phase), -np.sin(phase)], axis=0)
    wide = np.repeat(small, GROUP, axis=0).astype(np.float32)
    tall = (np.repeat(small.T, GROUP, axis=0) / seq_length).astype(np.float32)
    angle = 2 * np.pi * np.repeat(np.outer(4 * k + 1, b), GROUP, axis=0) / (4 * seq_length)
    turn = np.stack([np.cos(angle), np.sin(angle)]).astype(np.float32)
    inner = 2 * np.pi * (np.outer(b, b) % LANES) / LANES
    c, s = np.cos(inner), np.sin(inner)
    ahead = np.block([[c, -s], [s, c]]).astype(np.float32)
    back = np.block([[c, s], [-s, c]]).astype(np.float32)
    return (
        *split_table(wide),
        *split_table(tall),
        *split_table(ahead),
        *split_table(back),
        turn,
    )


def split(x):
    high = x.astype(jnp.bfloat16)
    return high, (x - high.astype(jnp.float32)).astype(jnp.bfloat16)


def dot3(first, second, dims=NN):
    def dot(x, y):
        return lax.dot_general(x, y, dims, preferred_element_type=jnp.float32)

    return dot(first[0], second[0]) + (dot(first[0], second[1]) + dot(first[1], second[0]))


def spread(small_ref, out_ref):
    rows, cols = out_ref.shape
    inner = small_ref.shape[1]
    pick = lax.broadcasted_iota(jnp.int32, (inner, cols), 1) // GROUP
    own = lax.broadcasted_iota(jnp.int32, (inner, cols), 0)
    picks = jnp.where(pick == own, 1.0, 0.0).astype(jnp.bfloat16)
    row_lane = lax.broadcasted_iota(jnp.int32, (rows, cols), 0) % GROUP
    col_lane = lax.broadcasted_iota(jnp.int32, (rows, cols), 1) % GROUP
    full = lax.dot_general(small_ref[...], picks, NN, preferred_element_type=jnp.float32)
    out_ref[...] = jnp.where(row_lane == col_lane, full, 0.0).astype(jnp.bfloat16)


def fused_kernel(devices, scale, *refs):
    x_hbm, vw_hbm, qw_hbm, f_hbm, g_hbm = refs[:5]
    table_hbm = refs[5:14]
    ig_out, fg_out, vg_out, qg_out = refs[14:18]
    x_ref, vw_ref, qw_ref, g_ref = refs[18:22]
    small_refs = refs[22:26]
    ahead_h, ahead_l, back_h, back_l, turn_ref = refs[26:31]
    wide_h, wide_l, tall_h, tall_l = refs[31:35]
    other_x, send_sig, in_sig, spec, out_sig, ret_sig, part, scat, red, gath = refs[35:45]
    ig_send, ig_recv, ssem, rsem, csend, crecv, lsem = refs[45:]
    me = lax.axis_index("seq")
    chan = lax.axis_index("chan")
    half, width = x_ref.shape
    pieces = width // LANES
    inner = 1 << (devices.bit_length() - 1) // 2
    outer = devices // inner
    rows = 2 * half // inner
    me_inner, me_outer = me % inner, me // inner

    def peer_of(i):
        peer, bit = me, 1
        while bit < devices:
            peer = peer + (i // bit) % 2 * (1 - 2 * (me // bit % 2)) * bit
            bit *= 2
        return peer

    barrier = pltpu.get_barrier_semaphore()

    def greet(i, carry):
        pl.semaphore_signal(
            barrier,
            inc=1,
            device_id={"seq": peer_of(devices - i)},
            device_id_type=pl.DeviceIdType.MESH,
        )
        return carry

    lax.fori_loop(1, devices, greet, 0)
    pl.semaphore_signal(
        barrier, inc=1, device_id={"chan": 1 - chan}, device_id_type=pl.DeviceIdType.MESH
    )

    loads = [
        pltpu.make_async_copy(src, dst, lsem.at[at])
        for at, (src, dst) in enumerate(
            zip(
                (x_hbm, vw_hbm, qw_hbm, g_hbm, *table_hbm),
                (x_ref, vw_ref, qw_ref, g_ref, *small_refs)
                + (ahead_h, ahead_l, back_h, back_l, turn_ref),
            )
        )
    ]
    for load in loads:
        load.start()
    own_f = pl.ds(pl.multiple_of(me * GROUP, GROUP), GROUP)
    keep_f = pltpu.make_async_copy(f_hbm.at[own_f, :], in_sig.at[0, me], lsem.at[len(loads)])
    keep_f.start()
    pl.semaphore_wait(barrier, devices)

    def exchange(index, src, dst):
        return pltpu.make_async_remote_copy(
            src_ref=src,
            dst_ref=dst,
            send_sem=csend.at[index],
            recv_sem=crecv.at[index],
            device_id={"chan": 1 - chan},
            device_id_type=pl.DeviceIdType.MESH,
        )

    def send_each(slot, src_of, dst, count=devices, stride=1):
        def step(i, carry):
            peer = peer_of((count - i) * stride)
            pltpu.make_async_remote_copy(
                src_ref=src_of(peer),
                dst_ref=dst,
                send_sem=ssem.at[slot],
                recv_sem=rsem.at[slot],
                device_id={"seq": peer},
                device_id_type=pl.DeviceIdType.MESH,
            ).start()
            return carry

        lax.fori_loop(1, count, step, 0)

    def drain(slot, ref, what):
        copy = pltpu.make_async_remote_copy(
            src_ref=ref,
            dst_ref=ref,
            send_sem=ssem.at[slot],
            recv_sem=rsem.at[slot],
            device_id={"seq": peer_of(1)},
            device_id_type=pl.DeviceIdType.MESH,
        )
        getattr(copy, what)()

    def group_rows(peer, count):
        return pl.ds(pl.multiple_of(peer * count, count), count)

    def out_way(slot, what):
        if what == "start":
            src = f_hbm if slot == 0 else send_sig.at[slot - 1]
            send_each(slot, lambda p: src.at[group_rows(p, GROUP), :], in_sig.at[slot, me])
        else:
            drain(slot, in_sig.at[slot, pl.ds(0, devices - 1)], what)

    def back_way(slot, what):
        if what == "start":
            send_each(
                3 + slot,
                lambda p: out_sig.at[slot, p],
                ret_sig.at[slot, group_rows(me, GROUP), :],
            )
        else:
            drain(3 + slot, out_sig.at[slot, pl.ds(0, devices - 1)], what)

    def scatter(slot, what):
        if what == "start":
            send_each(
                6 + slot,
                lambda p: part.at[slot, group_rows(p % inner, rows), :],
                scat.at[slot, me_inner],
                inner,
            )
        else:
            drain(6 + slot, scat.at[slot, pl.ds(0, inner - 1)], what)

    def swap(slot, what):
        if what == "start":
            send_each(
                8 + slot,
                lambda p: red.at[slot, me_outer],
                red.at[slot, me_outer],
                outer,
                inner,
            )
        else:
            drain(8 + slot, red.at[slot, pl.ds(0, outer - 1)], what)

    def gather(slot, what):
        mine = gath.at[slot, group_rows(me_inner, rows), :]
        if what == "start":
            send_each(10 + slot, lambda p: mine, mine, inner)
        else:
            drain(10 + slot, gath.at[slot, pl.ds(0, (inner - 1) * rows), :], what)

    give_x = exchange(0, x_hbm, other_x)
    give_x.start()
    out_way(0, "start")

    for load in loads[:3]:
        load.wait()
    own_rows = pl.ds(pl.multiple_of(chan * half, half), half)
    other_rows = pl.ds(pl.multiple_of((1 - chan) * half, half), half)
    own_x = split(x_ref[...])
    partial_value = dot3(split(vw_ref[own_rows, :].T), own_x)
    partial_query = dot3(split(qw_ref[own_rows, :].T), own_x)
    give_x.wait()

    far_x = split(other_x[...])
    send_sig[0] = partial_value + dot3(split(vw_ref[other_rows, :].T), far_x)
    out_way(1, "start")
    in_sig[1, me] = send_sig[0, group_rows(me, GROUP), :]
    query_proj = partial_query + dot3(split(qw_ref[other_rows, :].T), far_x)
    loads[3].wait()
    send_sig[1] = g_ref[...] * query_proj
    out_way(2, "start")
    in_sig[2, me] = send_sig[1, group_rows(me, GROUP), :]

    for load in loads[4:]:
        load.wait()
    for small_ref, out_ref in zip(small_refs, (wide_h, wide_l, tall_h, tall_l)):
        spread(small_ref, out_ref)
    keep_f.wait()
    wide = (wide_h[...], wide_l[...])
    tall = (tall_h[...], tall_l[...])
    ahead = (ahead_h[...], ahead_l[...])
    back = (back_h[...], back_l[...])
    cosine = turn_ref[0]
    sine = turn_ref[1]
    count = cosine.shape[0]

    def transform(slot):
        signal = jnp.concatenate(
            [
                in_sig[slot, source, :, piece * LANES : (piece + 1) * LANES]
                for source in range(devices)
                for piece in range(pieces)
            ],
            axis=0,
        )
        first = dot3(wide, split(signal))
        real, imag = first[:count], first[count:]
        turned = jnp.concatenate(
            [real * cosine + imag * sine, imag * cosine - real * sine], axis=1
        )
        spec[slot] = dot3(split(turned), ahead)

    def restore(first, second, conjugate, slot):
        real_a, imag_a = spec[first, :, :LANES], spec[first, :, LANES:]
        real_b, imag_b = spec[second, :, :LANES], spec[second, :, LANES:]
        if conjugate:
            imag_a = -imag_a
        product = jnp.concatenate(
            [real_a * real_b - imag_a * imag_b, real_a * imag_b + imag_a * real_b], axis=1
        )
        inner = dot3(split(product), back)
        real, imag = inner[:, :LANES], inner[:, LANES:]
        turned = jnp.concatenate(
            [real * cosine - imag * sine, imag * cosine + real * sine], axis=0
        )
        signal = dot3(tall, split(turned))
        if slot == 2:
            signal = signal * scale
        for target in range(devices):
            for piece in range(pieces):
                at = (target * pieces + piece) * GROUP
                out_sig[slot, target, :, piece * LANES : (piece + 1) * LANES] = signal[
                    at : at + GROUP
                ]
        back_way(slot, "start")
        ret_sig[slot, group_rows(me, GROUP), :] = out_sig[slot, me]

    out_way(0, "wait_recv")
    transform(0)
    out_way(1, "wait_recv")
    transform(1)
    restore(0, 1, False, 0)
    out_way(2, "wait_recv")
    transform(2)
    restore(0, 2, True, 1)
    restore(1, 2, True, 2)

    def weight_part(slot, grad):
        part[slot, own_rows, :] = dot3(own_x2, grad, NT)
        part[slot, other_rows, :] = dot3(far_x2, grad, NT)
        scatter(slot, "start")
        scat[slot, me_inner] = part[slot, group_rows(me_inner, rows), :]

    own_x2 = split(x_ref[...])
    far_x2 = split(other_x[...])
    back_way(0, "wait_recv")
    grad_query = split(g_ref[...] * ret_sig[0])
    weight_part(0, grad_query)
    near_grad = dot3(split(qw_ref[own_rows, :]), grad_query)
    far_grad = dot3(split(qw_ref[other_rows, :]), grad_query)

    def reduce_inner(slot):
        scatter(slot, "wait_recv")
        total = scat[slot, 0]
        for source in range(1, inner):
            total = total + scat[slot, source]
        red[slot, me_outer] = total
        swap(slot, "start")

    def reduce_outer(slot):
        swap(slot, "wait_recv")
        total = red[slot, 0]
        for source in range(1, outer):
            total = total + red[slot, source]
        gath[slot, group_rows(me_inner, rows), :] = total * scale
        gather(slot, "start")

    reduce_inner(0)
    back_way(1, "wait_recv")
    grad_value = split(ret_sig[1])
    weight_part(1, grad_value)
    ig_send[...] = far_grad + dot3(split(vw_ref[other_rows, :]), grad_value)
    give_ig = exchange(1, ig_send, ig_recv)
    give_ig.start()
    reduce_inner(1)
    near_grad = near_grad + dot3(split(vw_ref[own_rows, :]), grad_value)
    reduce_outer(0)
    give_ig.wait()
    ig_out[...] = near_grad + ig_recv[...]
    reduce_outer(1)
    back_way(2, "wait_recv")
    fg_out[...] = ret_sig[2]
    for slot, out in ((0, qg_out), (1, vg_out)):
        gather(slot, "wait_recv")
        out[...] = gath[slot]
    for slot in range(3):
        out_way(slot, "wait_send")
        back_way(slot, "wait_send")
    for slot in range(2):
        scatter(slot, "wait_send")
        swap(slot, "wait_send")
        gather(slot, "wait_send")


def finish_kernel(*refs):
    stores = [
        pltpu.make_async_copy(source, target, refs[8].at[at])
        for at, (source, target) in enumerate(zip(refs[:4], refs[4:8]))
    ]
    for store in stores:
        store.start()
    for store in stores:
        store.wait()


def fused_device(inputs, value_weight, query_weight, filters, grad_out):
    half, width = inputs.shape
    devices = lax.axis_size("seq")
    seq_length = width * devices
    depth = value_weight.shape[0]
    inner = 1 << (devices.bit_length() - 1) // 2
    outer = devices // inner
    rows = depth // inner
    tables = transform_tables(seq_length)
    count = seq_length // LANES * GROUP
    tables = [jnp.asarray(t) for t in tables]
    hbm = pl.BlockSpec(memory_space=pltpu.HBM)
    vmem = pl.BlockSpec(memory_space=pltpu.VMEM)
    f32, bf16 = jnp.float32, jnp.bfloat16
    outs = (
        jax.ShapeDtypeStruct((half, width), f32),
        jax.ShapeDtypeStruct((half, width), f32),
        jax.ShapeDtypeStruct((depth, half), f32),
        jax.ShapeDtypeStruct((depth, half), f32),
    )
    results = pl.pallas_call(
        functools.partial(fused_kernel, devices, 1.0 / math.sqrt(seq_length)),
        out_shape=tuple(pltpu.VMEM(out.shape, out.dtype) for out in outs),
        in_specs=[hbm] * (5 + len(tables)),
        out_specs=(vmem,) * 4,
        scratch_shapes=[
            pltpu.VMEM((half, width), f32),
            pltpu.VMEM((depth, half), f32),
            pltpu.VMEM((depth, half), f32),
            pltpu.VMEM((half, width), f32),
            *(pltpu.VMEM(t.shape, t.dtype) for t in tables),
            pltpu.VMEM((2 * count, count), bf16),
            pltpu.VMEM((2 * count, count), bf16),
            pltpu.VMEM((count, 2 * count), bf16),
            pltpu.VMEM((count, 2 * count), bf16),
            pltpu.VMEM((half, width), f32),
            pltpu.VMEM((2, half, width), f32),
            pltpu.VMEM((3, devices, GROUP, width), f32),
            pltpu.VMEM((3, count, 2 * LANES), f32),
            pltpu.VMEM((3, devices, GROUP, width), f32),
            pltpu.VMEM((3, half, width), f32),
            pltpu.VMEM((2, depth, half), f32),
            pltpu.VMEM((2, inner, rows, half), f32),
            pltpu.VMEM((2, outer, rows, half), f32),
            pltpu.VMEM((2, depth, half), f32),
            pltpu.VMEM((half, width), f32),
            pltpu.VMEM((half, width), f32),
            pltpu.SemaphoreType.DMA((12,)),
            pltpu.SemaphoreType.DMA((12,)),
            pltpu.SemaphoreType.DMA((2,)),
            pltpu.SemaphoreType.DMA((2,)),
            pltpu.SemaphoreType.DMA((5 + len(tables),)),
        ],
        compiler_params=pltpu.CompilerParams(
            collective_id=0, has_side_effects=True, vmem_limit_bytes=60 * 1024 * 1024
        ),
    )(inputs, value_weight, query_weight, filters, grad_out, *tables)
    return tuple(
        pl.pallas_call(
            finish_kernel,
            out_shape=outs,
            in_specs=[vmem] * 4,
            out_specs=(hbm,) * 4,
            scratch_shapes=[pltpu.SemaphoreType.DMA((4,))],
        )(*(pltpu.with_memory_space_constraint(r, pltpu.VMEM) for r in results))
    )


def on_device(inputs, value_weight, query_weight, filters, grad_out):
    channel_count, width = filters.shape
    devices = lax.axis_size("seq")
    fits = (
        channel_count == GROUP * devices
        and channel_count == inputs.shape[0]
        and lax.axis_size("chan") == 2
        and width % LANES == 0
        and channel_count % LANES == 0
        and devices & (devices - 1) == 0
        and value_weight.shape[0] % (GROUP * devices) == 0
    )
    body = fused_device if fits else per_device
    return body(inputs, value_weight, query_weight, filters, grad_out)


def solution(mesh):
    return jax.shard_map(
        on_device,
        mesh=mesh,
        in_specs=(
            P("chan", "seq"),
            P(None, "chan"),
            P(None, "chan"),
            P("chan", "seq"),
            P("chan", "seq"),
        ),
        out_specs=(P("chan", "seq"), P("chan", "seq"), P(None, "chan"), P(None, "chan")),
        check_vma=False,
    )
```

```python
import functools
import math

import jax
import jax.numpy as jnp
import numpy as np
from jax import lax
from jax.experimental import pallas as pl
from jax.experimental.pallas import tpu as pltpu
from jax.sharding import PartitionSpec as P

BLK = 64
LANES = 128
GROUP = 8


HIGHEST = lax.Precision.HIGHEST


def complex_table(row_count, col_count, period, direction):
    row_iota = lax.broadcasted_iota(jnp.int32, (row_count, col_count), 0)
    col_iota = lax.broadcasted_iota(jnp.int32, (row_count, col_count), 1)
    rotation = 2.0 * math.pi / period * (row_iota * col_iota % period).astype(jnp.float32)
    cosine = jnp.cos(rotation)
    sine_part = direction * jnp.sin(rotation)
    upper_rows = jnp.stack([cosine, sine_part], axis=1)
    lower_rows = jnp.stack([-sine_part, cosine], axis=1)
    return jnp.stack([upper_rows, lower_rows], axis=0)


def rotate(columns, cosine, sine_part):
    return jnp.stack(
        [columns[0] * cosine - columns[1] * sine_part, columns[0] * sine_part + columns[1] * cosine]
    )


def multiply(first_spec, second_spec, conjugate):
    imag_first = -first_spec[1] if conjugate else first_spec[1]
    return jnp.stack(
        [
            first_spec[0] * second_spec[0] - imag_first * second_spec[1],
            first_spec[0] * second_spec[1] + imag_first * second_spec[0],
        ]
    )


def block_angles(block_size, inner_size, seq_rows, direction):
    outer_iota = lax.broadcasted_iota(jnp.int32, (block_size, inner_size), 0)
    inner_iota = lax.broadcasted_iota(jnp.int32, (block_size, inner_size), 1)
    rotation = (
        direction
        * 2.0
        * math.pi
        / seq_rows
        * (outer_iota * inner_iota % seq_rows).astype(jnp.float32)
    )
    return (jnp.cos(rotation)[:, :, None], jnp.sin(rotation)[:, :, None])


def local_forward(columns, block_size):
    seq_rows = columns.shape[1]
    item_width = columns.shape[2]
    inner_size = seq_rows // block_size
    shaped = columns.reshape(2, block_size, inner_size, item_width)
    first_pass = jnp.einsum(
        "xabz,xayk->ykbz",
        shaped,
        complex_table(block_size, block_size, block_size, -1.0),
        precision=HIGHEST,
    )
    cosine, sine_part = block_angles(block_size, inner_size, seq_rows, -1.0)
    rotated = rotate(first_pass, cosine, sine_part)
    second = jnp.einsum(
        "ykbz,ybwm->wkmz",
        rotated,
        complex_table(inner_size, inner_size, inner_size, -1.0),
        precision=HIGHEST,
    )
    return second.reshape(2, seq_rows, item_width)


def local_inverse(columns, block_size):
    seq_rows = columns.shape[1]
    item_width = columns.shape[2]
    inner_size = seq_rows // block_size
    shaped = columns.reshape(2, block_size, inner_size, item_width)
    first_pass = jnp.einsum(
        "xkmz,xmyb->ykbz",
        shaped,
        complex_table(inner_size, inner_size, inner_size, 1.0),
        precision=HIGHEST,
    )
    cosine, sine_part = block_angles(block_size, inner_size, seq_rows, 1.0)
    rotated = rotate(first_pass, cosine, sine_part)
    second = jnp.einsum(
        "xkbz,xkya->yabz",
        rotated,
        complex_table(block_size, block_size, block_size, 1.0),
        precision=HIGHEST,
    )
    return second.reshape(2, seq_rows, item_width) * (1.0 / seq_rows)


def cross_transform(columns, dft_table):
    seq_rows = columns.shape[1]
    item_width = columns.shape[2]
    shaped = columns.reshape(2, 1, seq_rows, item_width)
    transformed = jnp.einsum(
        "xpjz,xpyk->ykjz",
        lax.all_to_all(shaped, "seq", split_axis=2, concat_axis=1, tiled=True),
        dft_table,
        precision=HIGHEST,
    )
    result = lax.all_to_all(transformed, "seq", split_axis=1, concat_axis=2, tiled=True)
    return result.reshape(2, seq_rows, item_width)


def shard_twiddle(columns, frequency, seq_length, direction):
    seq_rows = columns.shape[1]
    local_pos = jnp.arange(seq_rows, dtype=jnp.int32)
    rotation = (
        direction
        * 2.0
        * math.pi
        / seq_length
        * (local_pos * frequency % seq_length).astype(jnp.float32)
    )
    return rotate(columns, jnp.cos(rotation)[:, None], jnp.sin(rotation)[:, None])


def forward(columns, shard_index, devices, block_size):
    seq_length = columns.shape[1] * devices
    columns = cross_transform(columns, complex_table(devices, devices, devices, -1.0))
    columns = shard_twiddle(columns, shard_index, seq_length, -1.0)
    return local_forward(columns, block_size)


def inverse(columns, shard_index, devices, block_size):
    seq_length = columns.shape[1] * devices
    columns = local_inverse(columns, block_size)
    columns = shard_twiddle(columns, shard_index, seq_length, 1.0)
    columns = cross_transform(
        columns, complex_table(devices, devices, devices, 1.0) * (1.0 / devices)
    )
    return columns


def per_device(inputs, value_weight, query_weight, filters, grad_out):
    channel_count = filters.shape[0]
    seq_rows = filters.shape[1]
    devices = lax.axis_size("seq")
    shard_index = lax.axis_index("seq")
    seq_length = seq_rows * devices
    grad_scale = 1.0 / math.sqrt(seq_length)
    all_inputs = lax.all_gather(inputs, "chan", axis=0, tiled=True)
    projected = jnp.einsum("cd,ct->dt", value_weight, all_inputs, precision=HIGHEST)
    query_proj = jnp.einsum("cd,ct->dt", query_weight, all_inputs, precision=HIGHEST)
    gated_grad = grad_out * query_proj
    signals = jnp.stack([projected, filters, gated_grad])
    position = shard_index * seq_rows + jnp.arange(seq_rows, dtype=jnp.int32)
    twist_angle = 0.5 * math.pi / seq_length * position.astype(jnp.float32)
    cosine = jnp.cos(twist_angle)
    sine_part = jnp.sin(twist_angle)
    twisted = jnp.stack([signals * cosine, -signals * sine_part])
    columns = jnp.transpose(twisted, (0, 3, 1, 2)).reshape(2, seq_rows, 3 * channel_count)
    spectra = forward(columns, shard_index, devices, BLK).reshape(2, seq_rows, 3, channel_count)
    value_spec = spectra[:, :, 0]
    filter_spec = spectra[:, :, 1]
    grad_spec = spectra[:, :, 2]
    products = jnp.stack(
        [
            multiply(filter_spec, value_spec, False),
            multiply(filter_spec, grad_spec, True),
            multiply(value_spec, grad_spec, True),
        ],
        axis=2,
    )
    restored = inverse(
        products.reshape(2, seq_rows, 3 * channel_count), shard_index, devices, BLK
    ).reshape(2, seq_rows, 3, channel_count)
    combined = restored[0] * cosine[:, None, None] - restored[1] * sine_part[:, None, None]
    combined = jnp.transpose(combined, (1, 2, 0))
    convolved = combined[0]
    grad_value = combined[1]
    filter_grad = combined[2] * grad_scale
    grad_query = grad_out * convolved
    input_grad = lax.psum_scatter(
        jnp.dot(value_weight, grad_value, precision=HIGHEST, preferred_element_type=jnp.float32)
        + jnp.dot(query_weight, grad_query, precision=HIGHEST, preferred_element_type=jnp.float32),
        "chan",
        scatter_dimension=0,
        tiled=True,
    )
    partial_value = jnp.einsum("ct,dt->cd", all_inputs, grad_value, precision=HIGHEST) * grad_scale
    partial_query = jnp.einsum("ct,dt->cd", all_inputs, grad_query, precision=HIGHEST) * grad_scale
    value_gradient, query_gradient = lax.psum((partial_value, partial_query), "seq")
    return (input_grad, filter_grad, value_gradient, query_gradient)


NN = (((1,), (0,)), ((), ()))
NT = (((1,), (1,)), ((), ()))
scope = jax.named_scope


def split_table(table):
    high = table.astype(jnp.bfloat16)
    low = (table - high.astype(np.float32)).astype(jnp.bfloat16)
    return high, low


@functools.lru_cache(maxsize=None)
def transform_tables(seq_length):
    outer = seq_length // LANES
    k = np.arange(outer, dtype=np.float64)
    a = np.arange(outer, dtype=np.float64)
    b = np.arange(LANES, dtype=np.float64)
    phase = 2 * np.pi * np.outer(4 * k + 1, a) % (2 * np.pi * 4 * outer) / (4 * outer)
    small = np.concatenate([np.cos(phase), -np.sin(phase)], axis=0)
    wide_h, wide_l = split_table(small.astype(np.float32))
    tall_h, tall_l = split_table((small.T / seq_length).astype(np.float32))
    angle = 2 * np.pi * np.outer(4 * k + 1, b) / (4 * seq_length)
    turn = np.stack([np.cos(angle), np.sin(angle)]).astype(np.float32)
    inner = 2 * np.pi * (np.outer(b, b) % LANES) / LANES
    c, s = np.cos(inner), np.sin(inner)
    ahead_h, ahead_l = split_table(np.block([[c, -s], [s, c]]).astype(np.float32))
    back_h, back_l = split_table(np.block([[c, s], [-s, c]]).astype(np.float32))
    return (
        np.concatenate([wide_h, wide_l, wide_h, wide_l], axis=1),
        np.concatenate([tall_h, tall_l, tall_h, tall_l], axis=1),
        np.concatenate([ahead_h, ahead_h, ahead_l], axis=0),
        np.concatenate([back_h, back_h, back_l], axis=0),
        turn,
    )


def split(x):
    high = x.astype(jnp.bfloat16)
    return high, (x - high.astype(jnp.float32)).astype(jnp.bfloat16)


def dot3(first, second, dims=NN):
    def dot(x, y):
        return lax.dot_general(x, y, dims, preferred_element_type=jnp.float32)

    return dot(first[0], second[0]) + (dot(first[0], second[1]) + dot(first[1], second[0]))


def dot(first, second):
    return lax.dot_general(first, second, NN, preferred_element_type=jnp.float32)


def left3(x):
    high, low = split(x)
    return jnp.concatenate([high, low, high], axis=1)


def right4(x):
    high, low = split(x)
    return jnp.concatenate([high, high, low, low], axis=0)


def fused_kernel(devices, scale, *refs):
    x_hbm, vw_hbm, qw_hbm, f_hbm, g_hbm = refs[:5]
    table_hbm = refs[5:10]
    ig_out, fg_out, vg_out, qg_out = refs[10:14]
    x_ref, vw_ref, qw_ref, g_ref = refs[14:18]
    wide_ref, tall_ref, ahead_ref, back_ref, turn_ref = refs[18:23]
    other_x, f_sig, send_sig, in_sig, spec, out_sig, ret_sig, part, scat, red, gath = refs[23:34]
    ig_send, ig_recv, ssem, rsem, csend, crecv, lsem = refs[34:]
    me = lax.axis_index("seq")
    chan = lax.axis_index("chan")
    half, width = x_ref.shape
    pieces = width // LANES
    inner = 1 << (devices.bit_length() - 1) // 2
    outer = devices // inner
    rows = 2 * half // inner
    me_inner, me_outer = me % inner, me // inner

    def peer_of(i):
        peer, bit = me, 1
        while bit < devices:
            peer = peer + (i // bit) % 2 * (1 - 2 * (me // bit % 2)) * bit
            bit *= 2
        return peer

    barrier = pltpu.get_barrier_semaphore()

    def greet(i, carry):
        pl.semaphore_signal(
            barrier,
            inc=1,
            device_id={"seq": peer_of(devices - i)},
            device_id_type=pl.DeviceIdType.MESH,
        )
        return carry

    lax.fori_loop(1, devices, greet, 0)
    pl.semaphore_signal(
        barrier, inc=1, device_id={"chan": 1 - chan}, device_id_type=pl.DeviceIdType.MESH
    )

    def lanes(piece):
        return slice(piece * LANES, (piece + 1) * LANES)

    loads = [
        pltpu.make_async_copy(src, dst, lsem.at[at])
        for at, (src, dst) in enumerate(
            [
                *((f_hbm.at[:, lanes(piece)], f_sig.at[piece]) for piece in range(pieces)),
                (x_hbm, x_ref),
                (vw_hbm, vw_ref),
                (qw_hbm, qw_ref),
                (g_hbm, g_ref),
                *zip(table_hbm, (wide_ref, tall_ref, ahead_ref, back_ref, turn_ref)),
            ]
        )
    ]
    for load in loads:
        load.start()

    def wait_loads(count):
        for load in loads[:count]:
            load.wait()
        del loads[:count]

    pl.semaphore_wait(barrier, devices)

    def exchange(index, src, dst):
        return pltpu.make_async_remote_copy(
            src_ref=src,
            dst_ref=dst,
            send_sem=csend.at[index],
            recv_sem=crecv.at[index],
            device_id={"chan": 1 - chan},
            device_id_type=pl.DeviceIdType.MESH,
        )

    def send_each(slot, src_of, dst, count=devices, stride=1):
        def step(i, carry):
            peer = peer_of((count - i) * stride)
            pltpu.make_async_remote_copy(
                src_ref=src_of(peer),
                dst_ref=dst,
                send_sem=ssem.at[slot],
                recv_sem=rsem.at[slot],
                device_id={"seq": peer},
                device_id_type=pl.DeviceIdType.MESH,
            ).start()
            return carry

        lax.fori_loop(1, count, step, 0)

    def drain(slot, ref, what):
        copy = pltpu.make_async_remote_copy(
            src_ref=ref,
            dst_ref=ref,
            send_sem=ssem.at[slot],
            recv_sem=rsem.at[slot],
            device_id={"seq": peer_of(1)},
            device_id_type=pl.DeviceIdType.MESH,
        )
        getattr(copy, what)()

    def group_rows(peer, count):
        return pl.ds(pl.multiple_of(peer * count, count), count)

    def out_way(slot, what):
        if what == "start":
            src = f_sig if slot == 0 else send_sig.at[slot - 1]
            send_each(
                slot,
                lambda p: src.at[:, group_rows(p, GROUP), :],
                in_sig.at[slot, group_rows(me, pieces)],
            )
            in_sig[slot, group_rows(me, pieces)] = src[:, group_rows(me, GROUP), :]
        else:
            drain(slot, in_sig.at[slot, pl.ds(0, (devices - 1) * pieces)], what)

    def back_way(slot, what):
        if what == "start":
            send_each(
                3 + slot,
                lambda p: out_sig.at[slot, group_rows(p, pieces)],
                ret_sig.at[slot, :, group_rows(me, GROUP), :],
            )
            ret_sig[slot, :, group_rows(me, GROUP), :] = out_sig[slot, group_rows(me, pieces)]
        else:
            drain(3 + slot, out_sig.at[slot, pl.ds(0, (devices - 1) * pieces)], what)

    def scatter(slot, what):
        if what == "start":
            send_each(
                6 + slot,
                lambda p: part.at[slot, group_rows(p % inner, rows), :],
                scat.at[slot, me_inner],
                inner,
            )
        else:
            drain(6 + slot, scat.at[slot, pl.ds(0, inner - 1)], what)

    def swap(slot, what):
        if what == "start":
            send_each(
                8 + slot,
                lambda p: red.at[slot, me_outer],
                red.at[slot, me_outer],
                outer,
                inner,
            )
        else:
            drain(8 + slot, red.at[slot, pl.ds(0, outer - 1)], what)

    def gather(slot, what):
        mine = gath.at[slot, group_rows(me_inner, rows), :]
        if what == "start":
            send_each(10 + slot, lambda p: mine, mine, inner)
        else:
            drain(10 + slot, gath.at[slot, pl.ds(0, (inner - 1) * rows), :], what)

    give_x = exchange(0, x_hbm, other_x)
    give_x.start()
    with scope("load_f"):
        wait_loads(pieces)
    with scope("out0"):
        out_way(0, "start")

    wait_loads(3)
    own_rows = pl.ds(pl.multiple_of(chan * half, half), half)
    other_rows = pl.ds(pl.multiple_of((1 - chan) * half, half), half)
    own_x = split(x_ref[...])
    partial_value = dot3(split(vw_ref[own_rows, :].T), own_x)
    partial_query = dot3(split(qw_ref[own_rows, :].T), own_x)
    with scope("give_x"):
        give_x.wait()

    def stage(slot, value):
        for piece in range(pieces):
            send_sig[slot - 1, piece] = value[:, lanes(piece)]
        with scope("out"):
            out_way(slot, "start")

    far_x = split(other_x[...])
    stage(1, partial_value + dot3(split(vw_ref[other_rows, :].T), far_x))
    query_proj = partial_query + dot3(split(qw_ref[other_rows, :].T), far_x)
    wait_loads(1)
    stage(2, g_ref[...] * query_proj)

    wait_loads(len(loads))
    wide = wide_ref[...]
    tall = tall_ref[...]
    ahead = ahead_ref[...]
    back = back_ref[...]
    cosine = turn_ref[0]
    sine = turn_ref[1]
    outer_len = cosine.shape[0]

    def channel_rows(channel):
        return slice(channel * outer_len, (channel + 1) * outer_len)

    def channel_of(channel):
        return pl.ds(channel, outer_len, stride=GROUP)

    def transform(slot):
        signal = in_sig.at[slot].reshape(outer_len * GROUP, LANES)
        rows_of = []
        for pair in range(0, GROUP, 2):
            columns = jnp.concatenate(
                [signal[channel_of(channel), :] for channel in (pair, pair + 1)], axis=1
            )
            first = dot(wide, right4(columns))
            for at in range(2):
                real = first[:outer_len, lanes(at)]
                imag = first[outer_len:, lanes(at)]
                rows_of.append(
                    jnp.concatenate(
                        [real * cosine + imag * sine, imag * cosine - real * sine], axis=1
                    )
                )
        spec[slot] = dot(left3(jnp.concatenate(rows_of, axis=0)), ahead)

    def restore(first, second, conjugate, slot):
        real_a, imag_a = spec[first, :, :LANES], spec[first, :, LANES:]
        real_b, imag_b = spec[second, :, :LANES], spec[second, :, LANES:]
        if conjugate:
            imag_a = -imag_a
        product = jnp.concatenate(
            [real_a * real_b - imag_a * imag_b, real_a * imag_b + imag_a * real_b], axis=1
        )
        inverse = dot(left3(product), back)
        target = out_sig.at[slot].reshape(outer_len * GROUP, LANES)
        for pair in range(0, GROUP, 2):
            columns = []
            for channel in (pair, pair + 1):
                real = inverse[channel_rows(channel), :LANES]
                imag = inverse[channel_rows(channel), LANES:]
                columns.append(
                    jnp.concatenate(
                        [real * cosine - imag * sine, imag * cosine + real * sine], axis=0
                    )
                )
            signal = dot(tall, right4(jnp.concatenate(columns, axis=1)))
            if slot == 2:
                signal = signal * scale
            for at in range(2):
                target[channel_of(pair + at), :] = signal[:, lanes(at)]
        back_way(slot, "start")

    def returned(slot):
        return jnp.concatenate([ret_sig[slot, piece] for piece in range(pieces)], axis=1)

    with scope("wait0"):
        out_way(0, "wait_recv")
    with scope("t0"):
        transform(0)
    with scope("wait1"):
        out_way(1, "wait_recv")
    with scope("t1"):
        transform(1)
    with scope("r0"):
        restore(0, 1, False, 0)
    with scope("wait2"):
        out_way(2, "wait_recv")
    with scope("t2"):
        transform(2)
    with scope("r1"):
        restore(0, 2, True, 1)
    with scope("r2"):
        restore(1, 2, True, 2)

    def weight_part(slot, grad):
        part[slot, own_rows, :] = dot3(own_x2, grad, NT)
        part[slot, other_rows, :] = dot3(far_x2, grad, NT)
        scatter(slot, "start")
        scat[slot, me_inner] = part[slot, group_rows(me_inner, rows), :]

    own_x2 = split(x_ref[...])
    far_x2 = split(other_x[...])
    with scope("back0"):
        back_way(0, "wait_recv")
    grad_query = split(g_ref[...] * returned(0))
    weight_part(0, grad_query)
    near_grad = dot3(split(qw_ref[own_rows, :]), grad_query)
    far_grad = dot3(split(qw_ref[other_rows, :]), grad_query)

    def reduce_inner(slot):
        with scope(f"scat{slot}"):
            scatter(slot, "wait_recv")
        total = scat[slot, 0]
        for source in range(1, inner):
            total = total + scat[slot, source]
        red[slot, me_outer] = total
        swap(slot, "start")

    def reduce_outer(slot):
        with scope(f"swap{slot}"):
            swap(slot, "wait_recv")
        total = red[slot, 0]
        for source in range(1, outer):
            total = total + red[slot, source]
        gath[slot, group_rows(me_inner, rows), :] = total * scale
        gather(slot, "start")

    reduce_inner(0)
    with scope("back1"):
        back_way(1, "wait_recv")
    grad_value = split(returned(1))
    weight_part(1, grad_value)
    ig_send[...] = far_grad + dot3(split(vw_ref[other_rows, :]), grad_value)
    give_ig = exchange(1, ig_send, ig_recv)
    give_ig.start()
    reduce_inner(1)
    near_grad = near_grad + dot3(split(vw_ref[own_rows, :]), grad_value)
    reduce_outer(0)
    with scope("give_ig"):
        give_ig.wait()
    ig_out[...] = near_grad + ig_recv[...]
    reduce_outer(1)
    with scope("back2"):
        back_way(2, "wait_recv")
    fg_out[...] = returned(2)
    for slot, out in ((0, qg_out), (1, vg_out)):
        with scope(f"gather{slot}"):
            gather(slot, "wait_recv")
        out[...] = gath[slot]
    with scope("sends"):
        for slot in range(3):
            out_way(slot, "wait_send")
            back_way(slot, "wait_send")
        for slot in range(2):
            scatter(slot, "wait_send")
            swap(slot, "wait_send")
            gather(slot, "wait_send")


def finish_kernel(*refs):
    stores = [
        pltpu.make_async_copy(source, target, refs[8].at[at])
        for at, (source, target) in enumerate(zip(refs[:4], refs[4:8]))
    ]
    for store in stores:
        store.start()
    for store in stores:
        store.wait()


def fused_device(inputs, value_weight, query_weight, filters, grad_out):
    half, width = inputs.shape
    devices = lax.axis_size("seq")
    seq_length = width * devices
    depth = value_weight.shape[0]
    inner = 1 << (devices.bit_length() - 1) // 2
    outer = devices // inner
    rows = depth // inner
    tables = transform_tables(seq_length)
    pieces = width // LANES
    outer_len = seq_length // LANES
    tables = [jnp.asarray(t) for t in tables]
    hbm = pl.BlockSpec(memory_space=pltpu.HBM)
    vmem = pl.BlockSpec(memory_space=pltpu.VMEM)
    f32 = jnp.float32
    outs = (
        jax.ShapeDtypeStruct((half, width), f32),
        jax.ShapeDtypeStruct((half, width), f32),
        jax.ShapeDtypeStruct((depth, half), f32),
        jax.ShapeDtypeStruct((depth, half), f32),
    )
    results = pl.pallas_call(
        functools.partial(fused_kernel, devices, 1.0 / math.sqrt(seq_length)),
        out_shape=tuple(pltpu.VMEM(out.shape, out.dtype) for out in outs),
        in_specs=[hbm] * (5 + len(tables)),
        out_specs=(vmem,) * 4,
        scratch_shapes=[
            pltpu.VMEM((half, width), f32),
            pltpu.VMEM((depth, half), f32),
            pltpu.VMEM((depth, half), f32),
            pltpu.VMEM((half, width), f32),
            *(pltpu.VMEM(t.shape, t.dtype) for t in tables),
            pltpu.VMEM((half, width), f32),
            pltpu.VMEM((pieces, half, LANES), f32),
            pltpu.VMEM((2, pieces, half, LANES), f32),
            pltpu.VMEM((3, outer_len, GROUP, LANES), f32),
            pltpu.VMEM((3, outer_len * GROUP, 2 * LANES), f32),
            pltpu.VMEM((3, outer_len, GROUP, LANES), f32),
            pltpu.VMEM((3, pieces, half, LANES), f32),
            pltpu.VMEM((2, depth, half), f32),
            pltpu.VMEM((2, inner, rows, half), f32),
            pltpu.VMEM((2, outer, rows, half), f32),
            pltpu.VMEM((2, depth, half), f32),
            pltpu.VMEM((half, width), f32),
            pltpu.VMEM((half, width), f32),
            pltpu.SemaphoreType.DMA((12,)),
            pltpu.SemaphoreType.DMA((12,)),
            pltpu.SemaphoreType.DMA((2,)),
            pltpu.SemaphoreType.DMA((2,)),
            pltpu.SemaphoreType.DMA((4 + pieces + len(tables),)),
        ],
        compiler_params=pltpu.CompilerParams(
            collective_id=0, has_side_effects=True, vmem_limit_bytes=60 * 1024 * 1024
        ),
    )(inputs, value_weight, query_weight, filters, grad_out, *tables)
    return tuple(
        pl.pallas_call(
            finish_kernel,
            out_shape=outs,
            in_specs=[vmem] * 4,
            out_specs=(hbm,) * 4,
            scratch_shapes=[pltpu.SemaphoreType.DMA((4,))],
        )(*(pltpu.with_memory_space_constraint(r, pltpu.VMEM) for r in results))
    )


def on_device(inputs, value_weight, query_weight, filters, grad_out):
    channel_count, width = filters.shape
    devices = lax.axis_size("seq")
    fits = (
        channel_count == GROUP * devices
        and channel_count == inputs.shape[0]
        and lax.axis_size("chan") == 2
        and width % LANES == 0
        and channel_count % LANES == 0
        and devices & (devices - 1) == 0
        and (width * devices // LANES) % 16 == 0
        and value_weight.shape[0] % (GROUP * devices) == 0
    )
    body = fused_device if fits else per_device
    return body(inputs, value_weight, query_weight, filters, grad_out)


def solution(mesh):
    return jax.shard_map(
        on_device,
        mesh=mesh,
        in_specs=(
            P("chan", "seq"),
            P(None, "chan"),
            P(None, "chan"),
            P("chan", "seq"),
            P("chan", "seq"),
        ),
        out_specs=(P("chan", "seq"), P("chan", "seq"), P(None, "chan"), P(None, "chan")),
        check_vma=False,
    )
```

```python
import functools
import math

import jax
import jax.numpy as jnp
import numpy as np
from jax import lax
from jax.experimental import pallas as pl
from jax.experimental.pallas import tpu as pltpu
from jax.sharding import PartitionSpec as P

BLK = 64
LANES = 128
GROUP = 8


HIGHEST = lax.Precision.HIGHEST


def complex_table(row_count, col_count, period, direction):
    row_iota = lax.broadcasted_iota(jnp.int32, (row_count, col_count), 0)
    col_iota = lax.broadcasted_iota(jnp.int32, (row_count, col_count), 1)
    rotation = 2.0 * math.pi / period * (row_iota * col_iota % period).astype(jnp.float32)
    cosine = jnp.cos(rotation)
    sine_part = direction * jnp.sin(rotation)
    upper_rows = jnp.stack([cosine, sine_part], axis=1)
    lower_rows = jnp.stack([-sine_part, cosine], axis=1)
    return jnp.stack([upper_rows, lower_rows], axis=0)


def rotate(columns, cosine, sine_part):
    return jnp.stack(
        [columns[0] * cosine - columns[1] * sine_part, columns[0] * sine_part + columns[1] * cosine]
    )


def multiply(first_spec, second_spec, conjugate):
    imag_first = -first_spec[1] if conjugate else first_spec[1]
    return jnp.stack(
        [
            first_spec[0] * second_spec[0] - imag_first * second_spec[1],
            first_spec[0] * second_spec[1] + imag_first * second_spec[0],
        ]
    )


def block_angles(block_size, inner_size, seq_rows, direction):
    outer_iota = lax.broadcasted_iota(jnp.int32, (block_size, inner_size), 0)
    inner_iota = lax.broadcasted_iota(jnp.int32, (block_size, inner_size), 1)
    rotation = (
        direction
        * 2.0
        * math.pi
        / seq_rows
        * (outer_iota * inner_iota % seq_rows).astype(jnp.float32)
    )
    return (jnp.cos(rotation)[:, :, None], jnp.sin(rotation)[:, :, None])


def local_forward(columns, block_size):
    seq_rows = columns.shape[1]
    item_width = columns.shape[2]
    inner_size = seq_rows // block_size
    shaped = columns.reshape(2, block_size, inner_size, item_width)
    first_pass = jnp.einsum(
        "xabz,xayk->ykbz",
        shaped,
        complex_table(block_size, block_size, block_size, -1.0),
        precision=HIGHEST,
    )
    cosine, sine_part = block_angles(block_size, inner_size, seq_rows, -1.0)
    rotated = rotate(first_pass, cosine, sine_part)
    second = jnp.einsum(
        "ykbz,ybwm->wkmz",
        rotated,
        complex_table(inner_size, inner_size, inner_size, -1.0),
        precision=HIGHEST,
    )
    return second.reshape(2, seq_rows, item_width)


def local_inverse(columns, block_size):
    seq_rows = columns.shape[1]
    item_width = columns.shape[2]
    inner_size = seq_rows // block_size
    shaped = columns.reshape(2, block_size, inner_size, item_width)
    first_pass = jnp.einsum(
        "xkmz,xmyb->ykbz",
        shaped,
        complex_table(inner_size, inner_size, inner_size, 1.0),
        precision=HIGHEST,
    )
    cosine, sine_part = block_angles(block_size, inner_size, seq_rows, 1.0)
    rotated = rotate(first_pass, cosine, sine_part)
    second = jnp.einsum(
        "xkbz,xkya->yabz",
        rotated,
        complex_table(block_size, block_size, block_size, 1.0),
        precision=HIGHEST,
    )
    return second.reshape(2, seq_rows, item_width) * (1.0 / seq_rows)


def cross_transform(columns, dft_table):
    seq_rows = columns.shape[1]
    item_width = columns.shape[2]
    shaped = columns.reshape(2, 1, seq_rows, item_width)
    transformed = jnp.einsum(
        "xpjz,xpyk->ykjz",
        lax.all_to_all(shaped, "seq", split_axis=2, concat_axis=1, tiled=True),
        dft_table,
        precision=HIGHEST,
    )
    result = lax.all_to_all(transformed, "seq", split_axis=1, concat_axis=2, tiled=True)
    return result.reshape(2, seq_rows, item_width)


def shard_twiddle(columns, frequency, seq_length, direction):
    seq_rows = columns.shape[1]
    local_pos = jnp.arange(seq_rows, dtype=jnp.int32)
    rotation = (
        direction
        * 2.0
        * math.pi
        / seq_length
        * (local_pos * frequency % seq_length).astype(jnp.float32)
    )
    return rotate(columns, jnp.cos(rotation)[:, None], jnp.sin(rotation)[:, None])


def forward(columns, shard_index, devices, block_size):
    seq_length = columns.shape[1] * devices
    columns = cross_transform(columns, complex_table(devices, devices, devices, -1.0))
    columns = shard_twiddle(columns, shard_index, seq_length, -1.0)
    return local_forward(columns, block_size)


def inverse(columns, shard_index, devices, block_size):
    seq_length = columns.shape[1] * devices
    columns = local_inverse(columns, block_size)
    columns = shard_twiddle(columns, shard_index, seq_length, 1.0)
    columns = cross_transform(
        columns, complex_table(devices, devices, devices, 1.0) * (1.0 / devices)
    )
    return columns


def per_device(inputs, value_weight, query_weight, filters, grad_out):
    channel_count = filters.shape[0]
    seq_rows = filters.shape[1]
    devices = lax.axis_size("seq")
    shard_index = lax.axis_index("seq")
    seq_length = seq_rows * devices
    grad_scale = 1.0 / math.sqrt(seq_length)
    all_inputs = lax.all_gather(inputs, "chan", axis=0, tiled=True)
    projected = jnp.einsum("cd,ct->dt", value_weight, all_inputs, precision=HIGHEST)
    query_proj = jnp.einsum("cd,ct->dt", query_weight, all_inputs, precision=HIGHEST)
    gated_grad = grad_out * query_proj
    signals = jnp.stack([projected, filters, gated_grad])
    position = shard_index * seq_rows + jnp.arange(seq_rows, dtype=jnp.int32)
    twist_angle = 0.5 * math.pi / seq_length * position.astype(jnp.float32)
    cosine = jnp.cos(twist_angle)
    sine_part = jnp.sin(twist_angle)
    twisted = jnp.stack([signals * cosine, -signals * sine_part])
    columns = jnp.transpose(twisted, (0, 3, 1, 2)).reshape(2, seq_rows, 3 * channel_count)
    spectra = forward(columns, shard_index, devices, BLK).reshape(2, seq_rows, 3, channel_count)
    value_spec = spectra[:, :, 0]
    filter_spec = spectra[:, :, 1]
    grad_spec = spectra[:, :, 2]
    products = jnp.stack(
        [
            multiply(filter_spec, value_spec, False),
            multiply(filter_spec, grad_spec, True),
            multiply(value_spec, grad_spec, True),
        ],
        axis=2,
    )
    restored = inverse(
        products.reshape(2, seq_rows, 3 * channel_count), shard_index, devices, BLK
    ).reshape(2, seq_rows, 3, channel_count)
    combined = restored[0] * cosine[:, None, None] - restored[1] * sine_part[:, None, None]
    combined = jnp.transpose(combined, (1, 2, 0))
    convolved = combined[0]
    grad_value = combined[1]
    filter_grad = combined[2] * grad_scale
    grad_query = grad_out * convolved
    input_grad = lax.psum_scatter(
        jnp.dot(value_weight, grad_value, precision=HIGHEST, preferred_element_type=jnp.float32)
        + jnp.dot(query_weight, grad_query, precision=HIGHEST, preferred_element_type=jnp.float32),
        "chan",
        scatter_dimension=0,
        tiled=True,
    )
    partial_value = jnp.einsum("ct,dt->cd", all_inputs, grad_value, precision=HIGHEST) * grad_scale
    partial_query = jnp.einsum("ct,dt->cd", all_inputs, grad_query, precision=HIGHEST) * grad_scale
    value_gradient, query_gradient = lax.psum((partial_value, partial_query), "seq")
    return (input_grad, filter_grad, value_gradient, query_gradient)


NN = (((1,), (0,)), ((), ()))
NT = (((1,), (1,)), ((), ()))
scope = jax.named_scope


def split_table(table):
    high = table.astype(jnp.bfloat16)
    low = (table - high.astype(np.float32)).astype(jnp.bfloat16)
    return high, low


@functools.lru_cache(maxsize=None)
def transform_tables(seq_length):
    outer = seq_length // LANES
    k = np.arange(outer, dtype=np.float64)
    a = np.arange(outer, dtype=np.float64)
    b = np.arange(LANES, dtype=np.float64)
    phase = 2 * np.pi * np.outer(4 * k + 1, a) % (2 * np.pi * 4 * outer) / (4 * outer)
    small = np.concatenate([np.cos(phase), -np.sin(phase)], axis=0)
    wide_h, wide_l = split_table(small.astype(np.float32))
    tall_h, tall_l = split_table((small.T / seq_length).astype(np.float32))
    angle = 2 * np.pi * np.outer(4 * k + 1, b) / (4 * seq_length)
    turn = np.stack([np.cos(angle), np.sin(angle)]).astype(np.float32)
    inner = 2 * np.pi * (np.outer(b, b) % LANES) / LANES
    c, s = np.cos(inner), np.sin(inner)
    ahead_h, ahead_l = split_table(np.block([[c, -s], [s, c]]).astype(np.float32))
    back_h, back_l = split_table(np.block([[c, s], [-s, c]]).astype(np.float32))
    return (
        np.concatenate([wide_h, wide_l, wide_h, wide_l], axis=1),
        np.concatenate([tall_h, tall_l, tall_h, tall_l], axis=1),
        np.concatenate([ahead_h, ahead_h, ahead_l], axis=0),
        np.concatenate([back_h, back_h, back_l], axis=0),
        turn,
    )


def split(x):
    high = x.astype(jnp.bfloat16)
    return high, (x - high.astype(jnp.float32)).astype(jnp.bfloat16)


def dot3(first, second, dims=NN):
    def dot(x, y):
        return lax.dot_general(x, y, dims, preferred_element_type=jnp.float32)

    return dot(first[0], second[0]) + (dot(first[0], second[1]) + dot(first[1], second[0]))


def dot(first, second):
    return lax.dot_general(first, second, NN, preferred_element_type=jnp.float32)


def left3(x):
    high, low = split(x)
    return jnp.concatenate([high, low, high], axis=1)


def right4(x):
    high, low = split(x)
    return jnp.concatenate([high, high, low, low], axis=0)


def fused_kernel(devices, scale, *refs):
    x_hbm, vw_hbm, qw_hbm, f_hbm, g_hbm = refs[:5]
    table_hbm = refs[5:10]
    ig_out, fg_out, vg_out, qg_out = refs[10:14]
    x_ref, vw_ref, qw_ref, g_ref = refs[14:18]
    wide_ref, tall_ref, ahead_ref, back_ref, turn_ref = refs[18:23]
    other_x, f_sig, send_sig, in_sig, spec, out_sig, ret_sig, part, scat, red, gath = refs[23:34]
    ig_send, ig_recv, ssem, rsem, csend, crecv, lsem = refs[34:]
    me = lax.axis_index("seq")
    chan = lax.axis_index("chan")
    half, width = x_ref.shape
    pieces = width // LANES
    inner = devices // 2
    outer = devices // inner
    rows = 2 * half // inner
    me_inner, me_outer = me % inner, me // inner

    def peer_of(i):
        peer, bit = me, 1
        while bit < devices:
            peer = peer + (i // bit) % 2 * (1 - 2 * (me // bit % 2)) * bit
            bit *= 2
        return peer

    barrier = pltpu.get_barrier_semaphore()

    def greet(i, carry):
        pl.semaphore_signal(
            barrier,
            inc=1,
            device_id={"seq": peer_of(devices - i)},
            device_id_type=pl.DeviceIdType.MESH,
        )
        return carry

    lax.fori_loop(1, devices, greet, 0)
    pl.semaphore_signal(
        barrier, inc=1, device_id={"chan": 1 - chan}, device_id_type=pl.DeviceIdType.MESH
    )

    def lanes(piece):
        return slice(piece * LANES, (piece + 1) * LANES)

    loads = [
        pltpu.make_async_copy(src, dst, lsem.at[at])
        for at, (src, dst) in enumerate(
            [
                *((f_hbm.at[:, lanes(piece)], f_sig.at[piece]) for piece in range(pieces)),
                (x_hbm, x_ref),
                (vw_hbm, vw_ref),
                (qw_hbm, qw_ref),
                (g_hbm, g_ref),
                *zip(table_hbm, (wide_ref, tall_ref, ahead_ref, back_ref, turn_ref)),
            ]
        )
    ]
    for load in loads:
        load.start()

    def wait_loads(count):
        for load in loads[:count]:
            load.wait()
        del loads[:count]

    pl.semaphore_wait(barrier, devices)

    def exchange(index, src, dst):
        return pltpu.make_async_remote_copy(
            src_ref=src,
            dst_ref=dst,
            send_sem=csend.at[index],
            recv_sem=crecv.at[index],
            device_id={"chan": 1 - chan},
            device_id_type=pl.DeviceIdType.MESH,
        )

    def send_each(slot, src_of, dst, count=devices, stride=1, first=1):
        def step(i, carry):
            peer = peer_of((count - 1 - i) * stride)
            pltpu.make_async_remote_copy(
                src_ref=src_of(peer),
                dst_ref=dst,
                send_sem=ssem.at[slot],
                recv_sem=rsem.at[slot],
                device_id={"seq": peer},
                device_id_type=pl.DeviceIdType.MESH,
            ).start()
            return carry

        lax.fori_loop(0, count - first, step, 0)

    def drain(slot, ref, what):
        copy = pltpu.make_async_remote_copy(
            src_ref=ref,
            dst_ref=ref,
            send_sem=ssem.at[slot],
            recv_sem=rsem.at[slot],
            device_id={"seq": peer_of(1)},
            device_id_type=pl.DeviceIdType.MESH,
        )
        getattr(copy, what)()

    def group_rows(peer, count):
        return pl.ds(pl.multiple_of(peer * count, count), count)

    def out_way(slot, what):
        if what == "start":
            src = f_sig if slot == 0 else send_sig.at[slot - 1]
            send_each(
                slot,
                lambda p: src.at[:, group_rows(p, GROUP), :],
                in_sig.at[slot, group_rows(me, pieces)],
            )
            in_sig[slot, group_rows(me, pieces)] = src[:, group_rows(me, GROUP), :]
        else:
            drain(slot, in_sig.at[slot, pl.ds(0, (devices - 1) * pieces)], what)

    def back_way(slot, what, first=1, count=devices):
        if what == "start":
            send_each(
                3 + slot,
                lambda p: out_sig.at[slot, group_rows(p, pieces)],
                ret_sig.at[slot, :, group_rows(me, GROUP), :],
                count,
                1,
                first,
            )
            if first > 1:
                return
            ret_sig[slot, :, group_rows(me, GROUP), :] = out_sig[slot, group_rows(me, pieces)]
        else:
            drain(3 + slot, out_sig.at[slot, pl.ds(0, (devices - 1) * pieces)], what)

    def scatter(slot, what):
        if what == "start":
            send_each(
                6 + slot,
                lambda p: part.at[slot, group_rows(p % inner, rows), :],
                scat.at[slot, me_inner],
                inner,
            )
        else:
            drain(6 + slot, scat.at[slot, pl.ds(0, inner - 1)], what)

    def swap(slot, what):
        if what == "start":
            send_each(
                8 + slot,
                lambda p: red.at[slot, me_outer],
                red.at[slot, me_outer],
                outer,
                inner,
            )
        else:
            drain(8 + slot, red.at[slot, pl.ds(0, outer - 1)], what)

    def gather(slot, what):
        mine = gath.at[slot, group_rows(me_inner, rows), :]
        if what == "start":
            send_each(10 + slot, lambda p: mine, mine, inner)
        else:
            drain(10 + slot, gath.at[slot, pl.ds(0, (inner - 1) * rows), :], what)

    give_x = exchange(0, x_hbm, other_x)
    give_x.start()
    with scope("load_f"):
        wait_loads(pieces)
    with scope("out0"):
        out_way(0, "start")

    wait_loads(3)
    own_rows = pl.ds(pl.multiple_of(chan * half, half), half)
    other_rows = pl.ds(pl.multiple_of((1 - chan) * half, half), half)
    own_x = split(x_ref[...])
    partial_value = dot3(split(vw_ref[own_rows, :].T), own_x)
    partial_query = dot3(split(qw_ref[own_rows, :].T), own_x)
    with scope("give_x"):
        give_x.wait()

    def stage(slot, value):
        for piece in range(pieces):
            send_sig[slot - 1, piece] = value[:, lanes(piece)]
        with scope("out"):
            out_way(slot, "start")

    far_x = split(other_x[...])
    stage(1, partial_value + dot3(split(vw_ref[other_rows, :].T), far_x))
    query_proj = partial_query + dot3(split(qw_ref[other_rows, :].T), far_x)
    wait_loads(1)
    stage(2, g_ref[...] * query_proj)

    wait_loads(len(loads))
    wide = wide_ref[...]
    tall = tall_ref[...]
    ahead = ahead_ref[...]
    back = back_ref[...]
    cosine = turn_ref[0]
    sine = turn_ref[1]
    outer_len = cosine.shape[0]

    def channel_rows(channel):
        return slice(channel * outer_len, (channel + 1) * outer_len)

    def channel_of(channel):
        return pl.ds(channel, outer_len, stride=GROUP)

    def transform(slot):
        signal = in_sig.at[slot].reshape(outer_len * GROUP, LANES)
        rows_of = []
        for pair in range(0, GROUP, 2):
            columns = jnp.concatenate(
                [signal[channel_of(channel), :] for channel in (pair, pair + 1)], axis=1
            )
            first = dot(wide, right4(columns))
            for at in range(2):
                real = first[:outer_len, lanes(at)]
                imag = first[outer_len:, lanes(at)]
                rows_of.append(
                    jnp.concatenate(
                        [real * cosine + imag * sine, imag * cosine - real * sine], axis=1
                    )
                )
        spec[slot] = dot(left3(jnp.concatenate(rows_of, axis=0)), ahead)

    def restore(first, second, conjugate, slot):
        real_a, imag_a = spec[first, :, :LANES], spec[first, :, LANES:]
        real_b, imag_b = spec[second, :, :LANES], spec[second, :, LANES:]
        if conjugate:
            imag_a = -imag_a
        product = jnp.concatenate(
            [real_a * real_b - imag_a * imag_b, real_a * imag_b + imag_a * real_b], axis=1
        )
        inverse = dot(left3(product), back)
        target = out_sig.at[slot].reshape(outer_len * GROUP, LANES)
        for pair in range(0, GROUP, 2):
            columns = []
            for channel in (pair, pair + 1):
                real = inverse[channel_rows(channel), :LANES]
                imag = inverse[channel_rows(channel), LANES:]
                columns.append(
                    jnp.concatenate(
                        [real * cosine - imag * sine, imag * cosine + real * sine], axis=0
                    )
                )
            signal = dot(tall, right4(jnp.concatenate(columns, axis=1)))
            if slot == 2:
                signal = signal * scale
            for at in range(2):
                target[channel_of(pair + at), :] = signal[:, lanes(at)]

    def returned(slot):
        return jnp.concatenate([ret_sig[slot, piece] for piece in range(pieces)], axis=1)

    with scope("wait0"):
        out_way(0, "wait_recv")
    with scope("t0"):
        transform(0)
    with scope("wait1"):
        out_way(1, "wait_recv")
    with scope("t1"):
        transform(1)
    with scope("r0"):
        restore(0, 1, False, 0)
        back_way(0, "start")
    with scope("wait2"):
        out_way(2, "wait_recv")
    with scope("t2"):
        transform(2)
    with scope("r1"):
        restore(0, 2, True, 1)
        back_way(1, "start")
    with scope("r2"):
        restore(1, 2, True, 2)

    def weight_part(slot, grad):
        part[slot, own_rows, :] = dot3(own_x2, grad, NT)
        part[slot, other_rows, :] = dot3(far_x2, grad, NT)
        scatter(slot, "start")
        scat[slot, me_inner] = part[slot, group_rows(me_inner, rows), :]

    own_x2 = split(x_ref[...])
    far_x2 = split(other_x[...])
    with scope("back0"):
        back_way(0, "wait_recv")
    grad_query = split(g_ref[...] * returned(0))
    weight_part(0, grad_query)

    @pl.when(chan == 0)
    def _():
        back_way(2, "start", 12, 16)

    near_grad = dot3(split(qw_ref[own_rows, :]), grad_query)
    far_grad = dot3(split(qw_ref[other_rows, :]), grad_query)

    def reduce_inner(slot):
        with scope(f"scat{slot}"):
            scatter(slot, "wait_recv")
        total = scat[slot, 0]
        for source in range(1, inner):
            total = total + scat[slot, source]
        red[slot, me_outer] = total
        swap(slot, "start")

    def reduce_outer(slot):
        with scope(f"swap{slot}"):
            swap(slot, "wait_recv")
        total = red[slot, 0]
        for source in range(1, outer):
            total = total + red[slot, source]
        gath[slot, group_rows(me_inner, rows), :] = total * scale
        gather(slot, "start")

    with scope("back1"):
        back_way(1, "wait_recv")
    grad_value = split(returned(1))
    weight_part(1, grad_value)

    @pl.when(chan == 1)
    def _():
        back_way(2, "start", 12, 16)

    ig_send[...] = far_grad + dot3(split(vw_ref[other_rows, :]), grad_value)
    give_ig = exchange(1, ig_send, ig_recv)
    give_ig.start()
    reduce_inner(0)
    reduce_inner(1)
    back_way(2, "start", 1, 12)
    near_grad = near_grad + dot3(split(vw_ref[own_rows, :]), grad_value)
    reduce_outer(0)
    with scope("give_ig"):
        give_ig.wait()
    ig_out[...] = near_grad + ig_recv[...]
    reduce_outer(1)
    with scope("back2"):
        back_way(2, "wait_recv")
    fg_out[...] = returned(2)
    for slot, out in ((0, qg_out), (1, vg_out)):
        with scope(f"gather{slot}"):
            gather(slot, "wait_recv")
        out[...] = gath[slot]
    with scope("sends"):
        for slot in range(3):
            out_way(slot, "wait_send")
            back_way(slot, "wait_send")
        for slot in range(2):
            scatter(slot, "wait_send")
            swap(slot, "wait_send")
            gather(slot, "wait_send")


def finish_kernel(*refs):
    stores = [
        pltpu.make_async_copy(source, target, refs[8].at[at])
        for at, (source, target) in enumerate(zip(refs[:4], refs[4:8]))
    ]
    for store in stores:
        store.start()
    for store in stores:
        store.wait()


def fused_device(inputs, value_weight, query_weight, filters, grad_out):
    half, width = inputs.shape
    devices = lax.axis_size("seq")
    seq_length = width * devices
    depth = value_weight.shape[0]
    inner = devices // 2
    outer = devices // inner
    rows = depth // inner
    tables = transform_tables(seq_length)
    pieces = width // LANES
    outer_len = seq_length // LANES
    tables = [jnp.asarray(t) for t in tables]
    hbm = pl.BlockSpec(memory_space=pltpu.HBM)
    vmem = pl.BlockSpec(memory_space=pltpu.VMEM)
    f32 = jnp.float32
    outs = (
        jax.ShapeDtypeStruct((half, width), f32),
        jax.ShapeDtypeStruct((half, width), f32),
        jax.ShapeDtypeStruct((depth, half), f32),
        jax.ShapeDtypeStruct((depth, half), f32),
    )
    results = pl.pallas_call(
        functools.partial(fused_kernel, devices, 1.0 / math.sqrt(seq_length)),
        out_shape=tuple(pltpu.VMEM(out.shape, out.dtype) for out in outs),
        in_specs=[hbm] * (5 + len(tables)),
        out_specs=(vmem,) * 4,
        scratch_shapes=[
            pltpu.VMEM((half, width), f32),
            pltpu.VMEM((depth, half), f32),
            pltpu.VMEM((depth, half), f32),
            pltpu.VMEM((half, width), f32),
            *(pltpu.VMEM(t.shape, t.dtype) for t in tables),
            pltpu.VMEM((half, width), f32),
            pltpu.VMEM((pieces, half, LANES), f32),
            pltpu.VMEM((2, pieces, half, LANES), f32),
            pltpu.VMEM((3, outer_len, GROUP, LANES), f32),
            pltpu.VMEM((3, outer_len * GROUP, 2 * LANES), f32),
            pltpu.VMEM((3, outer_len, GROUP, LANES), f32),
            pltpu.VMEM((3, pieces, half, LANES), f32),
            pltpu.VMEM((2, depth, half), f32),
            pltpu.VMEM((2, inner, rows, half), f32),
            pltpu.VMEM((2, outer, rows, half), f32),
            pltpu.VMEM((2, depth, half), f32),
            pltpu.VMEM((half, width), f32),
            pltpu.VMEM((half, width), f32),
            pltpu.SemaphoreType.DMA((12,)),
            pltpu.SemaphoreType.DMA((12,)),
            pltpu.SemaphoreType.DMA((2,)),
            pltpu.SemaphoreType.DMA((2,)),
            pltpu.SemaphoreType.DMA((4 + pieces + len(tables),)),
        ],
        compiler_params=pltpu.CompilerParams(
            collective_id=0, has_side_effects=True, vmem_limit_bytes=60 * 1024 * 1024
        ),
    )(inputs, value_weight, query_weight, filters, grad_out, *tables)
    return tuple(
        pl.pallas_call(
            finish_kernel,
            out_shape=outs,
            in_specs=[vmem] * 4,
            out_specs=(hbm,) * 4,
            scratch_shapes=[pltpu.SemaphoreType.DMA((4,))],
        )(*(pltpu.with_memory_space_constraint(r, pltpu.VMEM) for r in results))
    )


def on_device(inputs, value_weight, query_weight, filters, grad_out):
    channel_count, width = filters.shape
    devices = lax.axis_size("seq")
    fits = (
        channel_count == GROUP * devices
        and channel_count == inputs.shape[0]
        and lax.axis_size("chan") == 2
        and width % LANES == 0
        and channel_count % LANES == 0
        and devices & (devices - 1) == 0
        and (width * devices // LANES) % 16 == 0
        and value_weight.shape[0] % (GROUP * devices) == 0
    )
    body = fused_device if fits else per_device
    return body(inputs, value_weight, query_weight, filters, grad_out)


def solution(mesh):
    return jax.shard_map(
        on_device,
        mesh=mesh,
        in_specs=(
            P("chan", "seq"),
            P(None, "chan"),
            P(None, "chan"),
            P("chan", "seq"),
            P("chan", "seq"),
        ),
        out_specs=(P("chan", "seq"), P("chan", "seq"), P(None, "chan"), P(None, "chan")),
        check_vma=False,
    )
```

```python
import functools
import math

import jax
import jax.numpy as jnp
import numpy as np
from jax import lax
from jax.experimental import pallas as pl
from jax.experimental.pallas import tpu as pltpu
from jax.sharding import PartitionSpec as P

BLK = 64
LANES = 128
GROUP = 8


HIGHEST = lax.Precision.HIGHEST


def complex_table(row_count, col_count, period, direction):
    row_iota = lax.broadcasted_iota(jnp.int32, (row_count, col_count), 0)
    col_iota = lax.broadcasted_iota(jnp.int32, (row_count, col_count), 1)
    rotation = 2.0 * math.pi / period * (row_iota * col_iota % period).astype(jnp.float32)
    cosine = jnp.cos(rotation)
    sine_part = direction * jnp.sin(rotation)
    upper_rows = jnp.stack([cosine, sine_part], axis=1)
    lower_rows = jnp.stack([-sine_part, cosine], axis=1)
    return jnp.stack([upper_rows, lower_rows], axis=0)


def rotate(columns, cosine, sine_part):
    return jnp.stack(
        [columns[0] * cosine - columns[1] * sine_part, columns[0] * sine_part + columns[1] * cosine]
    )


def multiply(first_spec, second_spec, conjugate):
    imag_first = -first_spec[1] if conjugate else first_spec[1]
    return jnp.stack(
        [
            first_spec[0] * second_spec[0] - imag_first * second_spec[1],
            first_spec[0] * second_spec[1] + imag_first * second_spec[0],
        ]
    )


def block_angles(block_size, inner_size, seq_rows, direction):
    outer_iota = lax.broadcasted_iota(jnp.int32, (block_size, inner_size), 0)
    inner_iota = lax.broadcasted_iota(jnp.int32, (block_size, inner_size), 1)
    rotation = (
        direction
        * 2.0
        * math.pi
        / seq_rows
        * (outer_iota * inner_iota % seq_rows).astype(jnp.float32)
    )
    return (jnp.cos(rotation)[:, :, None], jnp.sin(rotation)[:, :, None])


def local_forward(columns, block_size):
    seq_rows = columns.shape[1]
    item_width = columns.shape[2]
    inner_size = seq_rows // block_size
    shaped = columns.reshape(2, block_size, inner_size, item_width)
    first_pass = jnp.einsum(
        "xabz,xayk->ykbz",
        shaped,
        complex_table(block_size, block_size, block_size, -1.0),
        precision=HIGHEST,
    )
    cosine, sine_part = block_angles(block_size, inner_size, seq_rows, -1.0)
    rotated = rotate(first_pass, cosine, sine_part)
    second = jnp.einsum(
        "ykbz,ybwm->wkmz",
        rotated,
        complex_table(inner_size, inner_size, inner_size, -1.0),
        precision=HIGHEST,
    )
    return second.reshape(2, seq_rows, item_width)


def local_inverse(columns, block_size):
    seq_rows = columns.shape[1]
    item_width = columns.shape[2]
    inner_size = seq_rows // block_size
    shaped = columns.reshape(2, block_size, inner_size, item_width)
    first_pass = jnp.einsum(
        "xkmz,xmyb->ykbz",
        shaped,
        complex_table(inner_size, inner_size, inner_size, 1.0),
        precision=HIGHEST,
    )
    cosine, sine_part = block_angles(block_size, inner_size, seq_rows, 1.0)
    rotated = rotate(first_pass, cosine, sine_part)
    second = jnp.einsum(
        "xkbz,xkya->yabz",
        rotated,
        complex_table(block_size, block_size, block_size, 1.0),
        precision=HIGHEST,
    )
    return second.reshape(2, seq_rows, item_width) * (1.0 / seq_rows)


def cross_transform(columns, dft_table):
    seq_rows = columns.shape[1]
    item_width = columns.shape[2]
    shaped = columns.reshape(2, 1, seq_rows, item_width)
    transformed = jnp.einsum(
        "xpjz,xpyk->ykjz",
        lax.all_to_all(shaped, "seq", split_axis=2, concat_axis=1, tiled=True),
        dft_table,
        precision=HIGHEST,
    )
    result = lax.all_to_all(transformed, "seq", split_axis=1, concat_axis=2, tiled=True)
    return result.reshape(2, seq_rows, item_width)


def shard_twiddle(columns, frequency, seq_length, direction):
    seq_rows = columns.shape[1]
    local_pos = jnp.arange(seq_rows, dtype=jnp.int32)
    rotation = (
        direction
        * 2.0
        * math.pi
        / seq_length
        * (local_pos * frequency % seq_length).astype(jnp.float32)
    )
    return rotate(columns, jnp.cos(rotation)[:, None], jnp.sin(rotation)[:, None])


def forward(columns, shard_index, devices, block_size):
    seq_length = columns.shape[1] * devices
    columns = cross_transform(columns, complex_table(devices, devices, devices, -1.0))
    columns = shard_twiddle(columns, shard_index, seq_length, -1.0)
    return local_forward(columns, block_size)


def inverse(columns, shard_index, devices, block_size):
    seq_length = columns.shape[1] * devices
    columns = local_inverse(columns, block_size)
    columns = shard_twiddle(columns, shard_index, seq_length, 1.0)
    columns = cross_transform(
        columns, complex_table(devices, devices, devices, 1.0) * (1.0 / devices)
    )
    return columns


def per_device(inputs, value_weight, query_weight, filters, grad_out):
    channel_count = filters.shape[0]
    seq_rows = filters.shape[1]
    devices = lax.axis_size("seq")
    shard_index = lax.axis_index("seq")
    seq_length = seq_rows * devices
    grad_scale = 1.0 / math.sqrt(seq_length)
    all_inputs = lax.all_gather(inputs, "chan", axis=0, tiled=True)
    projected = jnp.einsum("cd,ct->dt", value_weight, all_inputs, precision=HIGHEST)
    query_proj = jnp.einsum("cd,ct->dt", query_weight, all_inputs, precision=HIGHEST)
    gated_grad = grad_out * query_proj
    signals = jnp.stack([projected, filters, gated_grad])
    position = shard_index * seq_rows + jnp.arange(seq_rows, dtype=jnp.int32)
    twist_angle = 0.5 * math.pi / seq_length * position.astype(jnp.float32)
    cosine = jnp.cos(twist_angle)
    sine_part = jnp.sin(twist_angle)
    twisted = jnp.stack([signals * cosine, -signals * sine_part])
    columns = jnp.transpose(twisted, (0, 3, 1, 2)).reshape(2, seq_rows, 3 * channel_count)
    spectra = forward(columns, shard_index, devices, BLK).reshape(2, seq_rows, 3, channel_count)
    value_spec = spectra[:, :, 0]
    filter_spec = spectra[:, :, 1]
    grad_spec = spectra[:, :, 2]
    products = jnp.stack(
        [
            multiply(filter_spec, value_spec, False),
            multiply(filter_spec, grad_spec, True),
            multiply(value_spec, grad_spec, True),
        ],
        axis=2,
    )
    restored = inverse(
        products.reshape(2, seq_rows, 3 * channel_count), shard_index, devices, BLK
    ).reshape(2, seq_rows, 3, channel_count)
    combined = restored[0] * cosine[:, None, None] - restored[1] * sine_part[:, None, None]
    combined = jnp.transpose(combined, (1, 2, 0))
    convolved = combined[0]
    grad_value = combined[1]
    filter_grad = combined[2] * grad_scale
    grad_query = grad_out * convolved
    input_grad = lax.psum_scatter(
        jnp.dot(value_weight, grad_value, precision=HIGHEST, preferred_element_type=jnp.float32)
        + jnp.dot(query_weight, grad_query, precision=HIGHEST, preferred_element_type=jnp.float32),
        "chan",
        scatter_dimension=0,
        tiled=True,
    )
    partial_value = jnp.einsum("ct,dt->cd", all_inputs, grad_value, precision=HIGHEST) * grad_scale
    partial_query = jnp.einsum("ct,dt->cd", all_inputs, grad_query, precision=HIGHEST) * grad_scale
    value_gradient, query_gradient = lax.psum((partial_value, partial_query), "seq")
    return (input_grad, filter_grad, value_gradient, query_gradient)


NN = (((1,), (0,)), ((), ()))
NT = (((1,), (1,)), ((), ()))
scope = jax.named_scope


def split_table(table):
    high = table.astype(jnp.bfloat16)
    low = (table - high.astype(np.float32)).astype(jnp.bfloat16)
    return high, low


@functools.lru_cache(maxsize=None)
def transform_tables(seq_length):
    outer = seq_length // LANES
    k = np.arange(outer, dtype=np.float64)
    a = np.arange(outer, dtype=np.float64)
    b = np.arange(LANES, dtype=np.float64)
    phase = 2 * np.pi * np.outer(4 * k + 1, a) % (2 * np.pi * 4 * outer) / (4 * outer)
    small = np.concatenate([np.cos(phase), -np.sin(phase)], axis=0)
    wide_h, wide_l = split_table(small.astype(np.float32))
    tall_h, tall_l = split_table((small.T / seq_length).astype(np.float32))
    angle = 2 * np.pi * np.outer(4 * k + 1, b) / (4 * seq_length)
    turn = np.stack([np.cos(angle), np.sin(angle)]).astype(np.float32)
    inner = 2 * np.pi * (np.outer(b, b) % LANES) / LANES
    c, s = np.cos(inner), np.sin(inner)
    ahead_h, ahead_l = split_table(np.block([[c, -s], [s, c]]).astype(np.float32))
    back_h, back_l = split_table(np.block([[c, s], [-s, c]]).astype(np.float32))
    first = slice(0, outer // 2)
    return (
        np.concatenate([wide_h, wide_l, wide_h, wide_l], axis=1),
        np.concatenate([tall_h, tall_l, tall_h, tall_l], axis=1),
        np.concatenate([t[:, first] for t in (wide_h, wide_l, wide_h, wide_l)], axis=1),
        np.concatenate([t[first] for t in (tall_h, tall_l, tall_h, tall_l)], axis=1),
        np.concatenate([ahead_h, ahead_h, ahead_l], axis=0),
        np.concatenate([back_h, back_h, back_l], axis=0),
        turn,
    )


def split(x):
    high = x.astype(jnp.bfloat16)
    return high, (x - high.astype(jnp.float32)).astype(jnp.bfloat16)


def dot3(first, second, dims=NN):
    def dot(x, y):
        return lax.dot_general(x, y, dims, preferred_element_type=jnp.float32)

    return dot(first[0], second[0]) + (dot(first[0], second[1]) + dot(first[1], second[0]))


def dot(first, second):
    return lax.dot_general(first, second, NN, preferred_element_type=jnp.float32)


def left3(x):
    high, low = split(x)
    return jnp.concatenate([high, low, high], axis=1)


def right4(x):
    high, low = split(x)
    return jnp.concatenate([high, high, low, low], axis=0)


def fused_kernel(devices, scale, *refs):
    x_hbm, vw_hbm, qw_hbm, f_hbm, g_hbm = refs[:5]
    table_hbm = refs[5:12]
    ig_out, fg_out, vg_out, qg_out = refs[12:16]
    x_ref, vw_ref, qw_ref, g_ref = refs[16:20]
    table_refs = refs[20:27]
    wide_ref, tall_ref, wide_loc_ref, tall_loc_ref, ahead_ref, back_ref, turn_ref = table_refs
    other_x, f_sig, send_sig, in_sig, spec, out_sig, ret_sig, part, scat, red, gath = refs[27:38]
    loc_sig, loc_spec, loc_out, loc_ret, ig_send, ig_recv = refs[38:44]
    ssem, rsem, csend, crecv, lsem = refs[44:]
    me = lax.axis_index("seq")
    chan = lax.axis_index("chan")
    half, width = x_ref.shape
    pieces = width // LANES
    inner = devices // 2
    outer = devices // inner
    rows = 2 * half // inner
    me_inner, me_outer = me % inner, me // inner
    near = devices // 2
    low = me < near
    high = me >= near

    steps = []
    while 1 << len(steps) < devices:
        bit = 1 << len(steps)
        steps.append((1 - 2 * (me // bit % 2)) * bit)

    def peer_of(i):
        return me + sum(step for at, step in enumerate(steps) if i >> at & 1)

    barrier = pltpu.get_barrier_semaphore()

    for index in reversed(range(1, devices)):
        pl.semaphore_signal(
            barrier,
            inc=1,
            device_id={"seq": peer_of(index)},
            device_id_type=pl.DeviceIdType.MESH,
        )
    pl.semaphore_signal(
        barrier, inc=1, device_id={"chan": 1 - chan}, device_id_type=pl.DeviceIdType.MESH
    )

    def lanes(piece):
        return slice(piece * LANES, (piece + 1) * LANES)

    loads = [
        pltpu.make_async_copy(src, dst, lsem.at[at])
        for at, (src, dst) in enumerate(
            [
                *(
                    (f_hbm.at[:, :, lanes(piece)], f_sig.at[:, piece])
                    for piece in range(pieces)
                ),
                (x_hbm, x_ref),
                (vw_hbm, vw_ref),
                (qw_hbm, qw_ref),
                (g_hbm, g_ref),
                *zip(table_hbm, table_refs),
            ]
        )
    ]
    for load in loads:
        load.start()

    def wait_loads(count):
        for load in loads[:count]:
            load.wait()
        del loads[:count]

    @pl.when(high)
    def _():
        in_sig[2, : near * pieces] = jnp.zeros_like(in_sig[2, : near * pieces])

    pl.semaphore_wait(barrier, devices)

    def exchange(index, src, dst):
        return pltpu.make_async_remote_copy(
            src_ref=src,
            dst_ref=dst,
            send_sem=csend.at[index],
            recv_sem=crecv.at[index],
            device_id={"chan": 1 - chan},
            device_id_type=pl.DeviceIdType.MESH,
        )

    def send_each(slot, src_of, dst, count=devices, stride=1, first=1):
        for index in reversed(range(first, count)):
            peer = peer_of(index * stride)
            pltpu.make_async_remote_copy(
                src_ref=src_of(peer),
                dst_ref=dst,
                send_sem=ssem.at[slot],
                recv_sem=rsem.at[slot],
                device_id={"seq": peer},
                device_id_type=pl.DeviceIdType.MESH,
            ).start()

    def drain(slot, ref, what):
        copy = pltpu.make_async_remote_copy(
            src_ref=ref,
            dst_ref=ref,
            send_sem=ssem.at[slot],
            recv_sem=rsem.at[slot],
            device_id={"seq": peer_of(1)},
            device_id_type=pl.DeviceIdType.MESH,
        )
        getattr(copy, what)()

    def group_rows(peer, count):
        return pl.ds(pl.multiple_of(peer * count, count), count)

    def messages(slot, count, what):
        drain(slot, in_sig.at[0, pl.ds(0, count * pieces)], what)

    def split_messages(slot, few, what):
        @pl.when(few)
        def _():
            messages(slot, near - 1, what)

        @pl.when(jnp.logical_not(few))
        def _():
            messages(slot, devices - 1, what)

    def out_way(slot, what):
        src = f_sig if slot == 0 else send_sig.at[slot - 1]
        mine = in_sig.at[slot, group_rows(me, pieces)]
        if what == "start":
            if slot < 2:
                send_each(slot, lambda p: src.at[p], mine, devices, 1, near)
            else:

                @pl.when(high)
                def _():
                    send_each(slot, lambda p: src.at[p], mine, devices, 1, near)

            send_each(slot, lambda p: src.at[p], mine, near)
            in_sig[slot, group_rows(me, pieces)] = src[me]

            @pl.when(low)
            def _():
                own = group_rows(me, pieces)
                send_each(12 + slot, lambda p: src.at[p + near], loc_sig.at[slot, own], near)
                loc_sig[slot, own] = src[me + near]

        elif slot < 2:
            messages(slot, devices - 1, what)
        else:
            split_messages(slot, high if what == "wait_recv" else low, what)

    def back_way(slot, what):
        def send(count, first):
            send_each(
                3 + slot,
                lambda p: out_sig.at[slot, group_rows(p, pieces)],
                ret_sig.at[slot, me],
                count,
                1,
                first,
            )

        if what == "start":
            if slot > 0:
                send(devices, near)
            else:

                @pl.when(low)
                def _():
                    send(devices, near)

            send(near, 1)
            ret_sig[slot, me] = out_sig[slot, group_rows(me, pieces)]
        elif slot > 0:
            messages(3 + slot, devices - 1, what)
        else:
            split_messages(3, low if what == "wait_recv" else high, what)

    def back_local(slot):
        own = ret_sig.at[0, me + near] if slot == 0 else loc_ret.at[slot - 1, me]
        send_each(
            15 + slot, lambda p: loc_out.at[slot, group_rows(p, pieces)], own, near
        )
        own[...] = loc_out[slot, group_rows(me, pieces)]

    def scatter(slot, what):
        if what == "start":
            send_each(
                6 + slot,
                lambda p: part.at[slot, group_rows(p % inner, rows), :],
                scat.at[slot, me_inner],
                inner,
            )
        else:
            drain(6 + slot, scat.at[slot, pl.ds(0, inner - 1)], what)

    def swap(slot, what):
        if what == "start":
            send_each(
                8 + slot,
                lambda p: red.at[slot, me_outer],
                red.at[slot, me_outer],
                outer,
                inner,
            )
        else:
            drain(8 + slot, red.at[slot, pl.ds(0, outer - 1)], what)

    def gather(slot, what):
        mine = gath.at[slot, group_rows(me_inner, rows), :]
        if what == "start":
            send_each(10 + slot, lambda p: mine, mine, inner)
        else:
            drain(10 + slot, gath.at[slot, pl.ds(0, (inner - 1) * rows), :], what)

    give_x = exchange(0, x_hbm, other_x)
    give_x.start()
    with scope("load_f"):
        wait_loads(pieces)
    with scope("out0"):
        out_way(0, "start")

    wait_loads(3)
    own_rows = pl.ds(pl.multiple_of(chan * half, half), half)
    other_rows = pl.ds(pl.multiple_of((1 - chan) * half, half), half)
    own_x = split(x_ref[...])
    partial_value = dot3(split(vw_ref[own_rows, :].T), own_x)
    partial_query = dot3(split(qw_ref[own_rows, :].T), own_x)
    with scope("give_x"):
        give_x.wait()

    def stage(slot, value):
        for piece in range(pieces):
            send_sig[slot - 1, :, piece] = value[:, lanes(piece)].reshape(devices, GROUP, LANES)
        with scope("out"):
            out_way(slot, "start")

    far_x = split(other_x[...])
    stage(1, partial_value + dot3(split(vw_ref[other_rows, :].T), far_x))
    query_proj = partial_query + dot3(split(qw_ref[other_rows, :].T), far_x)
    wait_loads(1)
    stage(2, g_ref[...] * query_proj)

    wait_loads(len(loads))
    wide = wide_ref[...]
    tall = tall_ref[...]
    ahead = ahead_ref[...]
    back = back_ref[...]
    cosine = turn_ref[0]
    sine = turn_ref[1]
    outer_len = cosine.shape[0]

    def channel_rows(channel):
        return slice(channel * outer_len, (channel + 1) * outer_len)

    def transform(source, table, target):
        count = source.shape[0]
        signal = source.reshape(count * GROUP, LANES)
        rows_of = []
        for pair in range(0, GROUP, 2):
            columns = jnp.concatenate(
                [
                    signal[pl.ds(channel, count, stride=GROUP), :]
                    for channel in (pair, pair + 1)
                ],
                axis=1,
            )
            first = dot(table, right4(columns))
            for at in range(2):
                real = first[:outer_len, lanes(at)]
                imag = first[outer_len:, lanes(at)]
                rows_of.append(
                    jnp.concatenate(
                        [real * cosine + imag * sine, imag * cosine - real * sine], axis=1
                    )
                )
        target[...] = dot(left3(jnp.concatenate(rows_of, axis=0)), ahead)

    def restore(first, second, conjugate, table, target, factor=None):
        count = target.shape[0]
        real_a, imag_a = first[:, :LANES], first[:, LANES:]
        real_b, imag_b = second[:, :LANES], second[:, LANES:]
        if conjugate:
            imag_a = -imag_a
        product = jnp.concatenate(
            [real_a * real_b - imag_a * imag_b, real_a * imag_b + imag_a * real_b], axis=1
        )
        inverse = dot(left3(product), back)
        result = target.reshape(count * GROUP, LANES)
        for pair in range(0, GROUP, 2):
            columns = []
            for channel in (pair, pair + 1):
                real = inverse[channel_rows(channel), :LANES]
                imag = inverse[channel_rows(channel), LANES:]
                columns.append(
                    jnp.concatenate(
                        [real * cosine - imag * sine, imag * cosine + real * sine], axis=0
                    )
                )
            signal = dot(table, right4(jnp.concatenate(columns, axis=1)))
            if factor is not None:
                signal = signal * factor
            for at in range(2):
                result[pl.ds(pair + at, count, stride=GROUP), :] = signal[:, lanes(at)]

    def returned(slot):
        return jnp.concatenate(
            [ret_sig[slot, :, piece].reshape(half, LANES) for piece in range(pieces)], axis=1
        )

    def local_transform(slot):
        with scope(f"locw{slot}"):
            messages(12 + slot, near - 1, "wait_recv")
        transform(loc_sig.at[slot], wide_loc_ref[...], loc_spec.at[slot])

    def local_restore(first, second, conjugate, slot, factor=None):
        restore(
            loc_spec.at[first],
            loc_spec.at[second],
            conjugate,
            tall_loc_ref[...],
            loc_out.at[slot],
            factor,
        )

    with scope("wait0"):
        out_way(0, "wait_recv")
    with scope("t0"):
        transform(in_sig.at[0], wide, spec.at[0])
    @pl.when(low)
    def _():
        local_transform(0)
        local_transform(1)
        with scope("locr0"):
            local_restore(0, 1, False, 0)
        back_local(0)

    with scope("wait1"):
        out_way(1, "wait_recv")
    with scope("t1"):
        transform(in_sig.at[1], wide, spec.at[1])
    with scope("r0"):
        restore(spec.at[0], spec.at[1], False, tall, out_sig.at[0])
        back_way(0, "start")

    @pl.when(low)
    def _():
        local_transform(2)
        with scope("locr1"):
            local_restore(0, 2, True, 1)
        back_local(1)
        with scope("locr2"):
            local_restore(1, 2, True, 2, scale)

    with scope("wait2"):
        out_way(2, "wait_recv")
    with scope("t2"):
        transform(in_sig.at[2], wide, spec.at[2])
    with scope("r1"):
        restore(spec.at[0], spec.at[2], True, tall, out_sig.at[1])
        back_way(1, "start")

    with scope("r2"):
        restore(spec.at[1], spec.at[2], True, tall, out_sig.at[2], scale)

    def back_ready(slot):
        with scope(f"back{slot}"):
            back_way(slot, "wait_recv")

            @pl.when(low)
            def _():
                messages(15 + slot, near - 1, "wait_recv")
                if slot > 0:
                    ret_sig[slot, near:] = ret_sig[slot, near:] + loc_ret[slot - 1]

    def weight_part(slot, grad):
        part[slot, own_rows, :] = dot3(own_x2, grad, NT)
        part[slot, other_rows, :] = dot3(far_x2, grad, NT)
        scatter(slot, "start")
        scat[slot, me_inner] = part[slot, group_rows(me_inner, rows), :]

    own_x2 = split(x_ref[...])
    far_x2 = split(other_x[...])
    back_ready(0)
    grad_query = split(g_ref[...] * returned(0))
    weight_part(0, grad_query)

    @pl.when(high)
    def _():
        back_way(2, "start")

    near_grad = dot3(split(qw_ref[own_rows, :]), grad_query)
    far_grad = dot3(split(qw_ref[other_rows, :]), grad_query)

    def reduce_inner(slot):
        with scope(f"scat{slot}"):
            scatter(slot, "wait_recv")
        total = scat[slot, 0]
        for source in range(1, inner):
            total = total + scat[slot, source]
        red[slot, me_outer] = total
        swap(slot, "start")

    def reduce_outer(slot):
        with scope(f"swap{slot}"):
            swap(slot, "wait_recv")
        total = red[slot, 0]
        for source in range(1, outer):
            total = total + red[slot, source]
        gath[slot, group_rows(me_inner, rows), :] = total * scale
        gather(slot, "start")

    back_ready(1)
    grad_value = split(returned(1))
    weight_part(1, grad_value)
    ig_send[...] = far_grad + dot3(split(vw_ref[other_rows, :]), grad_value)
    give_ig = exchange(1, ig_send, ig_recv)
    give_ig.start()
    reduce_inner(0)
    reduce_inner(1)

    @pl.when(low)
    def _():
        back_way(2, "start")
        back_local(2)

    near_grad = near_grad + dot3(split(vw_ref[own_rows, :]), grad_value)
    reduce_outer(0)
    with scope("give_ig"):
        give_ig.wait()
    ig_out[...] = near_grad + ig_recv[...]
    reduce_outer(1)
    back_ready(2)
    fg_out[...] = returned(2)
    for slot, out in ((0, qg_out), (1, vg_out)):
        with scope(f"gather{slot}"):
            gather(slot, "wait_recv")
        out[...] = gath[slot]
    with scope("sends"):
        for slot in range(3):
            out_way(slot, "wait_send")
            back_way(slot, "wait_send")
        for slot in range(2):
            scatter(slot, "wait_send")
            swap(slot, "wait_send")
            gather(slot, "wait_send")

        @pl.when(low)
        def _():
            for slot in range(12, 18):
                messages(slot, near - 1, "wait_send")


def finish_kernel(*refs):
    stores = [
        pltpu.make_async_copy(source, target, refs[8].at[at])
        for at, (source, target) in enumerate(zip(refs[:4], refs[4:8]))
    ]
    for store in stores:
        store.start()
    for store in stores:
        store.wait()


def fused_device(inputs, value_weight, query_weight, filters, grad_out):
    half, width = inputs.shape
    devices = lax.axis_size("seq")
    seq_length = width * devices
    depth = value_weight.shape[0]
    inner = devices // 2
    outer = devices // inner
    rows = depth // inner
    tables = transform_tables(seq_length)
    pieces = width // LANES
    outer_len = seq_length // LANES
    tables = [jnp.asarray(t) for t in tables]
    hbm = pl.BlockSpec(memory_space=pltpu.HBM)
    vmem = pl.BlockSpec(memory_space=pltpu.VMEM)
    f32 = jnp.float32
    outs = (
        jax.ShapeDtypeStruct((half, width), f32),
        jax.ShapeDtypeStruct((half, width), f32),
        jax.ShapeDtypeStruct((depth, half), f32),
        jax.ShapeDtypeStruct((depth, half), f32),
    )
    results = pl.pallas_call(
        functools.partial(fused_kernel, devices, 1.0 / math.sqrt(seq_length)),
        out_shape=tuple(pltpu.VMEM(out.shape, out.dtype) for out in outs),
        in_specs=[hbm] * (5 + len(tables)),
        out_specs=(vmem,) * 4,
        scratch_shapes=[
            pltpu.VMEM((half, width), f32),
            pltpu.VMEM((depth, half), f32),
            pltpu.VMEM((depth, half), f32),
            pltpu.VMEM((half, width), f32),
            *(pltpu.VMEM(t.shape, t.dtype) for t in tables),
            pltpu.VMEM((half, width), f32),
            pltpu.VMEM((devices, pieces, GROUP, LANES), f32),
            pltpu.VMEM((2, devices, pieces, GROUP, LANES), f32),
            pltpu.VMEM((3, outer_len, GROUP, LANES), f32),
            pltpu.VMEM((3, outer_len * GROUP, 2 * LANES), f32),
            pltpu.VMEM((3, outer_len, GROUP, LANES), f32),
            pltpu.VMEM((3, devices, pieces, GROUP, LANES), f32),
            pltpu.VMEM((2, depth, half), f32),
            pltpu.VMEM((2, inner, rows, half), f32),
            pltpu.VMEM((2, outer, rows, half), f32),
            pltpu.VMEM((2, depth, half), f32),
            pltpu.VMEM((3, outer_len // 2, GROUP, LANES), f32),
            pltpu.VMEM((3, outer_len * GROUP, 2 * LANES), f32),
            pltpu.VMEM((3, outer_len // 2, GROUP, LANES), f32),
            pltpu.VMEM((2, devices // 2, pieces, GROUP, LANES), f32),
            pltpu.VMEM((half, width), f32),
            pltpu.VMEM((half, width), f32),
            pltpu.SemaphoreType.DMA((18,)),
            pltpu.SemaphoreType.DMA((18,)),
            pltpu.SemaphoreType.DMA((2,)),
            pltpu.SemaphoreType.DMA((2,)),
            pltpu.SemaphoreType.DMA((4 + pieces + len(tables),)),
        ],
        compiler_params=pltpu.CompilerParams(
            collective_id=0, has_side_effects=True, vmem_limit_bytes=60 * 1024 * 1024
        ),
    )(
        inputs,
        value_weight,
        query_weight,
        filters.reshape(devices, GROUP, width),
        grad_out,
        *tables,
    )
    return tuple(
        pl.pallas_call(
            finish_kernel,
            out_shape=outs,
            in_specs=[vmem] * 4,
            out_specs=(hbm,) * 4,
            scratch_shapes=[pltpu.SemaphoreType.DMA((4,))],
        )(*(pltpu.with_memory_space_constraint(r, pltpu.VMEM) for r in results))
    )


def on_device(inputs, value_weight, query_weight, filters, grad_out):
    channel_count, width = filters.shape
    devices = lax.axis_size("seq")
    fits = (
        channel_count == GROUP * devices
        and channel_count == inputs.shape[0]
        and lax.axis_size("chan") == 2
        and width % LANES == 0
        and channel_count % LANES == 0
        and devices & (devices - 1) == 0
        and (width * devices // LANES) % 32 == 0
        and value_weight.shape[0] % (GROUP * devices) == 0
    )
    body = fused_device if fits else per_device
    return body(inputs, value_weight, query_weight, filters, grad_out)


def solution(mesh):
    return jax.shard_map(
        on_device,
        mesh=mesh,
        in_specs=(
            P("chan", "seq"),
            P(None, "chan"),
            P(None, "chan"),
            P("chan", "seq"),
            P("chan", "seq"),
        ),
        out_specs=(P("chan", "seq"), P("chan", "seq"), P(None, "chan"), P(None, "chan")),
        check_vma=False,
    )
```

```python
import functools
import math

import jax
import jax.numpy as jnp
import numpy as np
from jax import lax
from jax.experimental import pallas as pl
from jax.experimental.pallas import tpu as pltpu
from jax.sharding import PartitionSpec as P

BLK = 64
LANES = 128
GROUP = 8


HIGHEST = lax.Precision.HIGHEST


def complex_table(row_count, col_count, period, direction):
    row_iota = lax.broadcasted_iota(jnp.int32, (row_count, col_count), 0)
    col_iota = lax.broadcasted_iota(jnp.int32, (row_count, col_count), 1)
    rotation = 2.0 * math.pi / period * (row_iota * col_iota % period).astype(jnp.float32)
    cosine = jnp.cos(rotation)
    sine_part = direction * jnp.sin(rotation)
    upper_rows = jnp.stack([cosine, sine_part], axis=1)
    lower_rows = jnp.stack([-sine_part, cosine], axis=1)
    return jnp.stack([upper_rows, lower_rows], axis=0)


def rotate(columns, cosine, sine_part):
    return jnp.stack(
        [columns[0] * cosine - columns[1] * sine_part, columns[0] * sine_part + columns[1] * cosine]
    )


def multiply(first_spec, second_spec, conjugate):
    imag_first = -first_spec[1] if conjugate else first_spec[1]
    return jnp.stack(
        [
            first_spec[0] * second_spec[0] - imag_first * second_spec[1],
            first_spec[0] * second_spec[1] + imag_first * second_spec[0],
        ]
    )


def block_angles(block_size, inner_size, seq_rows, direction):
    outer_iota = lax.broadcasted_iota(jnp.int32, (block_size, inner_size), 0)
    inner_iota = lax.broadcasted_iota(jnp.int32, (block_size, inner_size), 1)
    rotation = (
        direction
        * 2.0
        * math.pi
        / seq_rows
        * (outer_iota * inner_iota % seq_rows).astype(jnp.float32)
    )
    return (jnp.cos(rotation)[:, :, None], jnp.sin(rotation)[:, :, None])


def local_forward(columns, block_size):
    seq_rows = columns.shape[1]
    item_width = columns.shape[2]
    inner_size = seq_rows // block_size
    shaped = columns.reshape(2, block_size, inner_size, item_width)
    first_pass = jnp.einsum(
        "xabz,xayk->ykbz",
        shaped,
        complex_table(block_size, block_size, block_size, -1.0),
        precision=HIGHEST,
    )
    cosine, sine_part = block_angles(block_size, inner_size, seq_rows, -1.0)
    rotated = rotate(first_pass, cosine, sine_part)
    second = jnp.einsum(
        "ykbz,ybwm->wkmz",
        rotated,
        complex_table(inner_size, inner_size, inner_size, -1.0),
        precision=HIGHEST,
    )
    return second.reshape(2, seq_rows, item_width)


def local_inverse(columns, block_size):
    seq_rows = columns.shape[1]
    item_width = columns.shape[2]
    inner_size = seq_rows // block_size
    shaped = columns.reshape(2, block_size, inner_size, item_width)
    first_pass = jnp.einsum(
        "xkmz,xmyb->ykbz",
        shaped,
        complex_table(inner_size, inner_size, inner_size, 1.0),
        precision=HIGHEST,
    )
    cosine, sine_part = block_angles(block_size, inner_size, seq_rows, 1.0)
    rotated = rotate(first_pass, cosine, sine_part)
    second = jnp.einsum(
        "xkbz,xkya->yabz",
        rotated,
        complex_table(block_size, block_size, block_size, 1.0),
        precision=HIGHEST,
    )
    return second.reshape(2, seq_rows, item_width) * (1.0 / seq_rows)


def cross_transform(columns, dft_table):
    seq_rows = columns.shape[1]
    item_width = columns.shape[2]
    shaped = columns.reshape(2, 1, seq_rows, item_width)
    transformed = jnp.einsum(
        "xpjz,xpyk->ykjz",
        lax.all_to_all(shaped, "seq", split_axis=2, concat_axis=1, tiled=True),
        dft_table,
        precision=HIGHEST,
    )
    result = lax.all_to_all(transformed, "seq", split_axis=1, concat_axis=2, tiled=True)
    return result.reshape(2, seq_rows, item_width)


def shard_twiddle(columns, frequency, seq_length, direction):
    seq_rows = columns.shape[1]
    local_pos = jnp.arange(seq_rows, dtype=jnp.int32)
    rotation = (
        direction
        * 2.0
        * math.pi
        / seq_length
        * (local_pos * frequency % seq_length).astype(jnp.float32)
    )
    return rotate(columns, jnp.cos(rotation)[:, None], jnp.sin(rotation)[:, None])


def forward(columns, shard_index, devices, block_size):
    seq_length = columns.shape[1] * devices
    columns = cross_transform(columns, complex_table(devices, devices, devices, -1.0))
    columns = shard_twiddle(columns, shard_index, seq_length, -1.0)
    return local_forward(columns, block_size)


def inverse(columns, shard_index, devices, block_size):
    seq_length = columns.shape[1] * devices
    columns = local_inverse(columns, block_size)
    columns = shard_twiddle(columns, shard_index, seq_length, 1.0)
    columns = cross_transform(
        columns, complex_table(devices, devices, devices, 1.0) * (1.0 / devices)
    )
    return columns


def per_device(inputs, value_weight, query_weight, filters, grad_out):
    channel_count = filters.shape[0]
    seq_rows = filters.shape[1]
    devices = lax.axis_size("seq")
    shard_index = lax.axis_index("seq")
    seq_length = seq_rows * devices
    grad_scale = 1.0 / math.sqrt(seq_length)
    all_inputs = lax.all_gather(inputs, "chan", axis=0, tiled=True)
    projected = jnp.einsum("cd,ct->dt", value_weight, all_inputs, precision=HIGHEST)
    query_proj = jnp.einsum("cd,ct->dt", query_weight, all_inputs, precision=HIGHEST)
    gated_grad = grad_out * query_proj
    signals = jnp.stack([projected, filters, gated_grad])
    position = shard_index * seq_rows + jnp.arange(seq_rows, dtype=jnp.int32)
    twist_angle = 0.5 * math.pi / seq_length * position.astype(jnp.float32)
    cosine = jnp.cos(twist_angle)
    sine_part = jnp.sin(twist_angle)
    twisted = jnp.stack([signals * cosine, -signals * sine_part])
    columns = jnp.transpose(twisted, (0, 3, 1, 2)).reshape(2, seq_rows, 3 * channel_count)
    spectra = forward(columns, shard_index, devices, BLK).reshape(2, seq_rows, 3, channel_count)
    value_spec = spectra[:, :, 0]
    filter_spec = spectra[:, :, 1]
    grad_spec = spectra[:, :, 2]
    products = jnp.stack(
        [
            multiply(filter_spec, value_spec, False),
            multiply(filter_spec, grad_spec, True),
            multiply(value_spec, grad_spec, True),
        ],
        axis=2,
    )
    restored = inverse(
        products.reshape(2, seq_rows, 3 * channel_count), shard_index, devices, BLK
    ).reshape(2, seq_rows, 3, channel_count)
    combined = restored[0] * cosine[:, None, None] - restored[1] * sine_part[:, None, None]
    combined = jnp.transpose(combined, (1, 2, 0))
    convolved = combined[0]
    grad_value = combined[1]
    filter_grad = combined[2] * grad_scale
    grad_query = grad_out * convolved
    input_grad = lax.psum_scatter(
        jnp.dot(value_weight, grad_value, precision=HIGHEST, preferred_element_type=jnp.float32)
        + jnp.dot(query_weight, grad_query, precision=HIGHEST, preferred_element_type=jnp.float32),
        "chan",
        scatter_dimension=0,
        tiled=True,
    )
    partial_value = jnp.einsum("ct,dt->cd", all_inputs, grad_value, precision=HIGHEST) * grad_scale
    partial_query = jnp.einsum("ct,dt->cd", all_inputs, grad_query, precision=HIGHEST) * grad_scale
    value_gradient, query_gradient = lax.psum((partial_value, partial_query), "seq")
    return (input_grad, filter_grad, value_gradient, query_gradient)


NN = (((1,), (0,)), ((), ()))
NT = (((1,), (1,)), ((), ()))
scope = jax.named_scope


def split_table(table):
    high = table.astype(jnp.bfloat16)
    low = (table - high.astype(np.float32)).astype(jnp.bfloat16)
    return high, low


@functools.lru_cache(maxsize=None)
def transform_tables(seq_length):
    outer = seq_length // LANES
    k = np.arange(outer, dtype=np.float64)
    a = np.arange(outer, dtype=np.float64)
    b = np.arange(LANES, dtype=np.float64)
    phase = 2 * np.pi * np.outer(4 * k + 1, a) % (2 * np.pi * 4 * outer) / (4 * outer)
    small = np.concatenate([np.cos(phase), -np.sin(phase)], axis=0)
    wide_h, wide_l = split_table(small.astype(np.float32))
    tall_h, tall_l = split_table((small.T / seq_length).astype(np.float32))
    angle = 2 * np.pi * np.outer(4 * k + 1, b) / (4 * seq_length)
    turn = np.stack([np.cos(angle), np.sin(angle)]).astype(np.float32)
    inner = 2 * np.pi * (np.outer(b, b) % LANES) / LANES
    c, s = np.cos(inner), np.sin(inner)
    ahead_h, ahead_l = split_table(np.block([[c, -s], [s, c]]).astype(np.float32))
    back_h, back_l = split_table(np.block([[c, s], [-s, c]]).astype(np.float32))
    first = slice(0, outer // 2)
    return (
        np.concatenate([wide_h, wide_l, wide_h, wide_l], axis=1),
        np.concatenate([tall_h, tall_l, tall_h, tall_l], axis=1),
        np.concatenate([t[:, first] for t in (wide_h, wide_l, wide_h, wide_l)], axis=1),
        np.concatenate([t[first] for t in (tall_h, tall_l, tall_h, tall_l)], axis=1),
        np.concatenate([ahead_h, ahead_h, ahead_l], axis=0),
        np.concatenate([back_h, back_h, back_l], axis=0),
        turn,
    )


def split(x):
    high = x.astype(jnp.bfloat16)
    return high, (x - high.astype(jnp.float32)).astype(jnp.bfloat16)


def dot3(first, second, dims=NN):
    def dot(x, y):
        return lax.dot_general(x, y, dims, preferred_element_type=jnp.float32)

    return dot(first[0], second[0]) + (dot(first[0], second[1]) + dot(first[1], second[0]))


def dot(first, second):
    return lax.dot_general(first, second, NN, preferred_element_type=jnp.float32)


def left3(x):
    high, low = split(x)
    return jnp.concatenate([high, low, high], axis=1)


def right4(x):
    high, low = split(x)
    return jnp.concatenate([high, high, low, low], axis=0)


def fused_kernel(devices, scale, *refs):
    x_hbm, vw_hbm, qw_hbm, f_hbm, g_hbm = refs[:5]
    table_hbm = refs[5:12]
    ig_out, fg_out, vg_out, qg_out = refs[12:16]
    x_ref, vw_ref, qw_ref, g_ref = refs[16:20]
    table_refs = refs[20:27]
    wide_ref, tall_ref, wide_loc_ref, tall_loc_ref, ahead_ref, back_ref, turn_ref = table_refs
    other_x, f_sig, send_sig, in_sig, spec, out_sig, ret_sig, part, scat, red, gath = refs[27:38]
    loc_sig, loc_spec, loc_out, loc_ret, ig_send, ig_recv = refs[38:44]
    ssem, rsem, csend, crecv, lsem = refs[44:]
    me = lax.axis_index("seq")
    chan = lax.axis_index("chan")
    half, width = x_ref.shape
    pieces = width // LANES
    inner = devices // 2
    outer = devices // inner
    rows = 2 * half // inner
    me_inner, me_outer = me % inner, me // inner
    near = devices // 2
    low = me < near
    high = me >= near

    steps = []
    while 1 << len(steps) < devices:
        bit = 1 << len(steps)
        steps.append((1 - 2 * (me // bit % 2)) * bit)

    def peer_of(i):
        return me + sum(step for at, step in enumerate(steps) if i >> at & 1)

    barrier = pltpu.get_barrier_semaphore()

    for index in reversed(range(1, devices)):
        pl.semaphore_signal(
            barrier,
            inc=1,
            device_id={"seq": peer_of(index)},
            device_id_type=pl.DeviceIdType.MESH,
        )
    pl.semaphore_signal(
        barrier, inc=1, device_id={"chan": 1 - chan}, device_id_type=pl.DeviceIdType.MESH
    )

    def lanes(piece):
        return slice(piece * LANES, (piece + 1) * LANES)

    loads = [
        pltpu.make_async_copy(src, dst, lsem.at[at])
        for at, (src, dst) in enumerate(
            [
                *(
                    (f_hbm.at[:, :, lanes(piece)], f_sig.at[:, piece])
                    for piece in range(pieces)
                ),
                (x_hbm, x_ref),
                (vw_hbm, vw_ref),
                (qw_hbm, qw_ref),
                (g_hbm, g_ref),
                *zip(table_hbm, table_refs),
            ]
        )
    ]
    for load in loads:
        load.start()

    def wait_loads(count):
        for load in loads[:count]:
            load.wait()
        del loads[:count]

    @pl.when(high)
    def _():
        in_sig[2, : near * pieces] = jnp.zeros_like(in_sig[2, : near * pieces])

    pl.semaphore_wait(barrier, devices)

    def exchange(index, src, dst):
        return pltpu.make_async_remote_copy(
            src_ref=src,
            dst_ref=dst,
            send_sem=csend.at[index],
            recv_sem=crecv.at[index],
            device_id={"chan": 1 - chan},
            device_id_type=pl.DeviceIdType.MESH,
        )

    def send_each(slot, src_of, dst, count=devices, stride=1, first=1):
        for index in reversed(range(first, count)):
            peer = peer_of(index * stride)
            pltpu.make_async_remote_copy(
                src_ref=src_of(peer),
                dst_ref=dst,
                send_sem=ssem.at[slot],
                recv_sem=rsem.at[slot],
                device_id={"seq": peer},
                device_id_type=pl.DeviceIdType.MESH,
            ).start()

    def drain(slot, ref, what):
        copy = pltpu.make_async_remote_copy(
            src_ref=ref,
            dst_ref=ref,
            send_sem=ssem.at[slot],
            recv_sem=rsem.at[slot],
            device_id={"seq": peer_of(1)},
            device_id_type=pl.DeviceIdType.MESH,
        )
        getattr(copy, what)()

    def group_rows(peer, count):
        return pl.ds(pl.multiple_of(peer * count, count), count)

    def messages(slot, count, what):
        drain(slot, in_sig.at[0, pl.ds(0, count * pieces)], what)

    def split_messages(slot, few, what):
        @pl.when(few)
        def _():
            messages(slot, near - 1, what)

        @pl.when(jnp.logical_not(few))
        def _():
            messages(slot, devices - 1, what)

    def out_way(slot, what):
        src = f_sig if slot == 0 else send_sig.at[slot - 1]
        mine = in_sig.at[slot, group_rows(me, pieces)]
        if what == "start":
            if slot < 2:
                send_each(slot, lambda p: src.at[p], mine, devices, 1, near)
            else:

                @pl.when(high)
                def _():
                    send_each(slot, lambda p: src.at[p], mine, devices, 1, near)

            send_each(slot, lambda p: src.at[p], mine, near)
            in_sig[slot, group_rows(me, pieces)] = src[me]

            @pl.when(low)
            def _():
                own = group_rows(me, pieces)
                send_each(12 + slot, lambda p: src.at[p + near], loc_sig.at[slot, own], near)
                loc_sig[slot, own] = src[me + near]

        elif slot < 2:
            messages(slot, devices - 1, what)
        else:
            split_messages(slot, high if what == "wait_recv" else low, what)

    def back_way(slot, what):
        def send(count, first):
            send_each(
                3 + slot,
                lambda p: out_sig.at[slot, group_rows(p, pieces)],
                ret_sig.at[slot, me],
                count,
                1,
                first,
            )

        if what == "start":
            if slot > 0:
                send(devices, near)
            else:

                @pl.when(low)
                def _():
                    send(devices, near)

            send(near, 1)
            ret_sig[slot, me] = out_sig[slot, group_rows(me, pieces)]
        elif slot > 0:
            messages(3 + slot, devices - 1, what)
        else:
            split_messages(3, low if what == "wait_recv" else high, what)

    def back_local(slot):
        own = ret_sig.at[0, me + near] if slot == 0 else loc_ret.at[slot - 1, me]
        send_each(
            15 + slot, lambda p: loc_out.at[slot, group_rows(p, pieces)], own, near
        )
        own[...] = loc_out[slot, group_rows(me, pieces)]

    def scatter(slot, what):
        if what == "start":
            send_each(
                6 + slot,
                lambda p: part.at[slot, group_rows(p % inner, rows), :],
                scat.at[slot, me_inner],
                inner,
            )
        else:
            drain(6 + slot, scat.at[slot, pl.ds(0, inner - 1)], what)

    def swap(slot, what):
        if what == "start":
            send_each(
                8 + slot,
                lambda p: red.at[slot, me_outer],
                red.at[slot, me_outer],
                outer,
                inner,
            )
        else:
            drain(8 + slot, red.at[slot, pl.ds(0, outer - 1)], what)

    def gather(slot, what):
        mine = gath.at[slot, group_rows(me_inner, rows), :]
        if what == "start":
            send_each(10 + slot, lambda p: mine, mine, inner)
        else:
            drain(10 + slot, gath.at[slot, pl.ds(0, (inner - 1) * rows), :], what)

    give_x = exchange(0, x_hbm, other_x)
    give_x.start()
    with scope("load_f"):
        wait_loads(pieces)
    with scope("out0"):
        out_way(0, "start")

    wait_loads(3)
    own_rows = pl.ds(pl.multiple_of(chan * half, half), half)
    other_rows = pl.ds(pl.multiple_of((1 - chan) * half, half), half)
    own_x = split(x_ref[...])
    partial_value = dot3(split(vw_ref[own_rows, :].T), own_x)
    partial_query = dot3(split(qw_ref[own_rows, :].T), own_x)
    with scope("give_x"):
        give_x.wait()

    def stage(slot, value):
        for piece in range(pieces):
            send_sig[slot - 1, :, piece] = value[:, lanes(piece)].reshape(devices, GROUP, LANES)
        with scope("out"):
            out_way(slot, "start")

    far_x = split(other_x[...])
    stage(1, partial_value + dot3(split(vw_ref[other_rows, :].T), far_x))
    query_proj = partial_query + dot3(split(qw_ref[other_rows, :].T), far_x)
    wait_loads(1)
    stage(2, g_ref[...] * query_proj)

    wait_loads(len(loads))
    wide = wide_ref[...]
    tall = tall_ref[...]
    ahead = ahead_ref[...]
    back = back_ref[...]
    cosine = turn_ref[0]
    sine = turn_ref[1]
    outer_len = cosine.shape[0]

    def channel_rows(channel):
        return slice(channel * outer_len, (channel + 1) * outer_len)

    def transform(source, table, target):
        count = source.shape[0]
        signal = source.reshape(count * GROUP, LANES)
        rows_of = []
        for pair in range(0, GROUP, 2):
            columns = jnp.concatenate(
                [
                    signal[pl.ds(channel, count, stride=GROUP), :]
                    for channel in (pair, pair + 1)
                ],
                axis=1,
            )
            first = dot(table, right4(columns))
            for at in range(2):
                real = first[:outer_len, lanes(at)]
                imag = first[outer_len:, lanes(at)]
                rows_of.append(
                    jnp.concatenate(
                        [real * cosine + imag * sine, imag * cosine - real * sine], axis=1
                    )
                )
        target[...] = dot(left3(jnp.concatenate(rows_of, axis=0)), ahead)

    def restore(first, second, conjugate, table, target, factor=None):
        count = target.shape[0]
        real_a, imag_a = first[:, :LANES], first[:, LANES:]
        real_b, imag_b = second[:, :LANES], second[:, LANES:]
        if conjugate:
            imag_a = -imag_a
        product = jnp.concatenate(
            [real_a * real_b - imag_a * imag_b, real_a * imag_b + imag_a * real_b], axis=1
        )
        inverse = dot(left3(product), back)
        result = target.reshape(count * GROUP, LANES)
        for pair in range(0, GROUP, 2):
            columns = []
            for channel in (pair, pair + 1):
                real = inverse[channel_rows(channel), :LANES]
                imag = inverse[channel_rows(channel), LANES:]
                columns.append(
                    jnp.concatenate(
                        [real * cosine - imag * sine, imag * cosine + real * sine], axis=0
                    )
                )
            signal = dot(table, right4(jnp.concatenate(columns, axis=1)))
            if factor is not None:
                signal = signal * factor
            for at in range(2):
                result[pl.ds(pair + at, count, stride=GROUP), :] = signal[:, lanes(at)]

    def returned(slot):
        return jnp.concatenate(
            [ret_sig[slot, :, piece].reshape(half, LANES) for piece in range(pieces)], axis=1
        )

    def local_transform(slot):
        with scope(f"locw{slot}"):
            messages(12 + slot, near - 1, "wait_recv")
        transform(loc_sig.at[slot], wide_loc_ref[...], loc_spec.at[slot])

    def local_restore(first, second, conjugate, slot, factor=None):
        restore(
            loc_spec.at[first],
            loc_spec.at[second],
            conjugate,
            tall_loc_ref[...],
            loc_out.at[slot],
            factor,
        )

    with scope("wait0"):
        out_way(0, "wait_recv")
    with scope("t0"):
        transform(in_sig.at[0], wide, spec.at[0])
    @pl.when(low)
    def _():
        local_transform(0)
        local_transform(1)
        with scope("locr0"):
            local_restore(0, 1, False, 0)
        back_local(0)

    with scope("wait1"):
        out_way(1, "wait_recv")
    with scope("t1"):
        transform(in_sig.at[1], wide, spec.at[1])
    with scope("r0"):
        restore(spec.at[0], spec.at[1], False, tall, out_sig.at[0])
        back_way(0, "start")

    @pl.when(low)
    def _():
        local_transform(2)
        with scope("locr1"):
            local_restore(0, 2, True, 1)
        back_local(1)
        with scope("locr2"):
            local_restore(1, 2, True, 2, scale)

    with scope("wait2"):
        out_way(2, "wait_recv")
    with scope("t2"):
        transform(in_sig.at[2], wide, spec.at[2])
    with scope("r1"):
        restore(spec.at[0], spec.at[2], True, tall, out_sig.at[1])
        back_way(1, "start")

    with scope("r2"):
        restore(spec.at[1], spec.at[2], True, tall, out_sig.at[2], scale)

    @pl.when(high & (chan == 1))
    def _():
        back_way(2, "start")


    def back_ready(slot):
        with scope(f"back{slot}"):
            back_way(slot, "wait_recv")

            @pl.when(low)
            def _():
                messages(15 + slot, near - 1, "wait_recv")
                if slot > 0:
                    ret_sig[slot, near:] = ret_sig[slot, near:] + loc_ret[slot - 1]

    def weight_part(slot, grad):
        part[slot, own_rows, :] = dot3(own_x2, grad, NT)
        part[slot, other_rows, :] = dot3(far_x2, grad, NT)
        scatter(slot, "start")
        scat[slot, me_inner] = part[slot, group_rows(me_inner, rows), :]

    own_x2 = split(x_ref[...])
    far_x2 = split(other_x[...])
    back_ready(0)
    grad_query = split(g_ref[...] * returned(0))
    weight_part(0, grad_query)

    @pl.when(high & (chan == 0))
    def _():
        back_way(2, "start")


    near_grad = dot3(split(qw_ref[own_rows, :]), grad_query)
    far_grad = dot3(split(qw_ref[other_rows, :]), grad_query)

    def reduce_inner(slot):
        with scope(f"scat{slot}"):
            scatter(slot, "wait_recv")
        total = scat[slot, 0]
        for source in range(1, inner):
            total = total + scat[slot, source]
        red[slot, me_outer] = total
        swap(slot, "start")

    def reduce_outer(slot):
        with scope(f"swap{slot}"):
            swap(slot, "wait_recv")
        total = red[slot, 0]
        for source in range(1, outer):
            total = total + red[slot, source]
        gath[slot, group_rows(me_inner, rows), :] = total * scale
        gather(slot, "start")

    back_ready(1)
    grad_value = split(returned(1))
    weight_part(1, grad_value)
    ig_send[...] = far_grad + dot3(split(vw_ref[other_rows, :]), grad_value)
    give_ig = exchange(1, ig_send, ig_recv)
    give_ig.start()
    reduce_inner(0)
    reduce_inner(1)

    @pl.when(low)
    def _():
        back_way(2, "start")
        back_local(2)


    near_grad = near_grad + dot3(split(vw_ref[own_rows, :]), grad_value)
    reduce_outer(0)
    with scope("give_ig"):
        give_ig.wait()
    ig_out[...] = near_grad + ig_recv[...]
    reduce_outer(1)
    back_ready(2)
    fg_out[...] = returned(2)
    for slot, out in ((0, qg_out), (1, vg_out)):
        with scope(f"gather{slot}"):
            gather(slot, "wait_recv")
        out[...] = gath[slot]
    with scope("sends"):
        for slot in range(3):
            out_way(slot, "wait_send")
            back_way(slot, "wait_send")
        for slot in range(2):
            scatter(slot, "wait_send")
            swap(slot, "wait_send")
            gather(slot, "wait_send")

        @pl.when(low)
        def _():
            for slot in range(12, 18):
                messages(slot, near - 1, "wait_send")


def finish_kernel(*refs):
    stores = [
        pltpu.make_async_copy(source, target, refs[8].at[at])
        for at, (source, target) in enumerate(zip(refs[:4], refs[4:8]))
    ]
    for store in stores:
        store.start()
    for store in stores:
        store.wait()


def fused_device(inputs, value_weight, query_weight, filters, grad_out):
    half, width = inputs.shape
    devices = lax.axis_size("seq")
    seq_length = width * devices
    depth = value_weight.shape[0]
    inner = devices // 2
    outer = devices // inner
    rows = depth // inner
    tables = transform_tables(seq_length)
    pieces = width // LANES
    outer_len = seq_length // LANES
    tables = [jnp.asarray(t) for t in tables]
    hbm = pl.BlockSpec(memory_space=pltpu.HBM)
    vmem = pl.BlockSpec(memory_space=pltpu.VMEM)
    f32 = jnp.float32
    outs = (
        jax.ShapeDtypeStruct((half, width), f32),
        jax.ShapeDtypeStruct((half, width), f32),
        jax.ShapeDtypeStruct((depth, half), f32),
        jax.ShapeDtypeStruct((depth, half), f32),
    )
    results = pl.pallas_call(
        functools.partial(fused_kernel, devices, 1.0 / math.sqrt(seq_length)),
        out_shape=tuple(pltpu.VMEM(out.shape, out.dtype) for out in outs),
        in_specs=[hbm] * (5 + len(tables)),
        out_specs=(vmem,) * 4,
        scratch_shapes=[
            pltpu.VMEM((half, width), f32),
            pltpu.VMEM((depth, half), f32),
            pltpu.VMEM((depth, half), f32),
            pltpu.VMEM((half, width), f32),
            *(pltpu.VMEM(t.shape, t.dtype) for t in tables),
            pltpu.VMEM((half, width), f32),
            pltpu.VMEM((devices, pieces, GROUP, LANES), f32),
            pltpu.VMEM((2, devices, pieces, GROUP, LANES), f32),
            pltpu.VMEM((3, outer_len, GROUP, LANES), f32),
            pltpu.VMEM((3, outer_len * GROUP, 2 * LANES), f32),
            pltpu.VMEM((3, outer_len, GROUP, LANES), f32),
            pltpu.VMEM((3, devices, pieces, GROUP, LANES), f32),
            pltpu.VMEM((2, depth, half), f32),
            pltpu.VMEM((2, inner, rows, half), f32),
            pltpu.VMEM((2, outer, rows, half), f32),
            pltpu.VMEM((2, depth, half), f32),
            pltpu.VMEM((3, outer_len // 2, GROUP, LANES), f32),
            pltpu.VMEM((3, outer_len * GROUP, 2 * LANES), f32),
            pltpu.VMEM((3, outer_len // 2, GROUP, LANES), f32),
            pltpu.VMEM((2, devices // 2, pieces, GROUP, LANES), f32),
            pltpu.VMEM((half, width), f32),
            pltpu.VMEM((half, width), f32),
            pltpu.SemaphoreType.DMA((18,)),
            pltpu.SemaphoreType.DMA((18,)),
            pltpu.SemaphoreType.DMA((2,)),
            pltpu.SemaphoreType.DMA((2,)),
            pltpu.SemaphoreType.DMA((4 + pieces + len(tables),)),
        ],
        compiler_params=pltpu.CompilerParams(
            collective_id=0, has_side_effects=True, vmem_limit_bytes=60 * 1024 * 1024
        ),
    )(
        inputs,
        value_weight,
        query_weight,
        filters.reshape(devices, GROUP, width),
        grad_out,
        *tables,
    )
    return tuple(
        pl.pallas_call(
            finish_kernel,
            out_shape=outs,
            in_specs=[vmem] * 4,
            out_specs=(hbm,) * 4,
            scratch_shapes=[pltpu.SemaphoreType.DMA((4,))],
        )(*(pltpu.with_memory_space_constraint(r, pltpu.VMEM) for r in results))
    )


def on_device(inputs, value_weight, query_weight, filters, grad_out):
    channel_count, width = filters.shape
    devices = lax.axis_size("seq")
    fits = (
        channel_count == GROUP * devices
        and channel_count == inputs.shape[0]
        and lax.axis_size("chan") == 2
        and width % LANES == 0
        and channel_count % LANES == 0
        and devices & (devices - 1) == 0
        and (width * devices // LANES) % 32 == 0
        and value_weight.shape[0] % (GROUP * devices) == 0
    )
    body = fused_device if fits else per_device
    return body(inputs, value_weight, query_weight, filters, grad_out)


def solution(mesh):
    return jax.shard_map(
        on_device,
        mesh=mesh,
        in_specs=(
            P("chan", "seq"),
            P(None, "chan"),
            P(None, "chan"),
            P("chan", "seq"),
            P("chan", "seq"),
        ),
        out_specs=(P("chan", "seq"), P("chan", "seq"), P(None, "chan"), P(None, "chan")),
        check_vma=False,
    )
```

```python
import functools
import math

import jax
import jax.numpy as jnp
import numpy as np
from jax import lax
from jax.experimental import pallas as pl
from jax.experimental.pallas import tpu as pltpu
from jax.sharding import PartitionSpec as P

BLK = 64
LANES = 128
GROUP = 8


HIGHEST = lax.Precision.HIGHEST


def complex_table(row_count, col_count, period, direction):
    row_iota = lax.broadcasted_iota(jnp.int32, (row_count, col_count), 0)
    col_iota = lax.broadcasted_iota(jnp.int32, (row_count, col_count), 1)
    rotation = 2.0 * math.pi / period * (row_iota * col_iota % period).astype(jnp.float32)
    cosine = jnp.cos(rotation)
    sine_part = direction * jnp.sin(rotation)
    upper_rows = jnp.stack([cosine, sine_part], axis=1)
    lower_rows = jnp.stack([-sine_part, cosine], axis=1)
    return jnp.stack([upper_rows, lower_rows], axis=0)


def rotate(columns, cosine, sine_part):
    return jnp.stack(
        [columns[0] * cosine - columns[1] * sine_part, columns[0] * sine_part + columns[1] * cosine]
    )


def multiply(first_spec, second_spec, conjugate):
    imag_first = -first_spec[1] if conjugate else first_spec[1]
    return jnp.stack(
        [
            first_spec[0] * second_spec[0] - imag_first * second_spec[1],
            first_spec[0] * second_spec[1] + imag_first * second_spec[0],
        ]
    )


def block_angles(block_size, inner_size, seq_rows, direction):
    outer_iota = lax.broadcasted_iota(jnp.int32, (block_size, inner_size), 0)
    inner_iota = lax.broadcasted_iota(jnp.int32, (block_size, inner_size), 1)
    rotation = (
        direction
        * 2.0
        * math.pi
        / seq_rows
        * (outer_iota * inner_iota % seq_rows).astype(jnp.float32)
    )
    return (jnp.cos(rotation)[:, :, None], jnp.sin(rotation)[:, :, None])


def local_forward(columns, block_size):
    seq_rows = columns.shape[1]
    item_width = columns.shape[2]
    inner_size = seq_rows // block_size
    shaped = columns.reshape(2, block_size, inner_size, item_width)
    first_pass = jnp.einsum(
        "xabz,xayk->ykbz",
        shaped,
        complex_table(block_size, block_size, block_size, -1.0),
        precision=HIGHEST,
    )
    cosine, sine_part = block_angles(block_size, inner_size, seq_rows, -1.0)
    rotated = rotate(first_pass, cosine, sine_part)
    second = jnp.einsum(
        "ykbz,ybwm->wkmz",
        rotated,
        complex_table(inner_size, inner_size, inner_size, -1.0),
        precision=HIGHEST,
    )
    return second.reshape(2, seq_rows, item_width)


def local_inverse(columns, block_size):
    seq_rows = columns.shape[1]
    item_width = columns.shape[2]
    inner_size = seq_rows // block_size
    shaped = columns.reshape(2, block_size, inner_size, item_width)
    first_pass = jnp.einsum(
        "xkmz,xmyb->ykbz",
        shaped,
        complex_table(inner_size, inner_size, inner_size, 1.0),
        precision=HIGHEST,
    )
    cosine, sine_part = block_angles(block_size, inner_size, seq_rows, 1.0)
    rotated = rotate(first_pass, cosine, sine_part)
    second = jnp.einsum(
        "xkbz,xkya->yabz",
        rotated,
        complex_table(block_size, block_size, block_size, 1.0),
        precision=HIGHEST,
    )
    return second.reshape(2, seq_rows, item_width) * (1.0 / seq_rows)


def cross_transform(columns, dft_table):
    seq_rows = columns.shape[1]
    item_width = columns.shape[2]
    shaped = columns.reshape(2, 1, seq_rows, item_width)
    transformed = jnp.einsum(
        "xpjz,xpyk->ykjz",
        lax.all_to_all(shaped, "seq", split_axis=2, concat_axis=1, tiled=True),
        dft_table,
        precision=HIGHEST,
    )
    result = lax.all_to_all(transformed, "seq", split_axis=1, concat_axis=2, tiled=True)
    return result.reshape(2, seq_rows, item_width)


def shard_twiddle(columns, frequency, seq_length, direction):
    seq_rows = columns.shape[1]
    local_pos = jnp.arange(seq_rows, dtype=jnp.int32)
    rotation = (
        direction
        * 2.0
        * math.pi
        / seq_length
        * (local_pos * frequency % seq_length).astype(jnp.float32)
    )
    return rotate(columns, jnp.cos(rotation)[:, None], jnp.sin(rotation)[:, None])


def forward(columns, shard_index, devices, block_size):
    seq_length = columns.shape[1] * devices
    columns = cross_transform(columns, complex_table(devices, devices, devices, -1.0))
    columns = shard_twiddle(columns, shard_index, seq_length, -1.0)
    return local_forward(columns, block_size)


def inverse(columns, shard_index, devices, block_size):
    seq_length = columns.shape[1] * devices
    columns = local_inverse(columns, block_size)
    columns = shard_twiddle(columns, shard_index, seq_length, 1.0)
    columns = cross_transform(
        columns, complex_table(devices, devices, devices, 1.0) * (1.0 / devices)
    )
    return columns


def per_device(inputs, value_weight, query_weight, filters, grad_out):
    channel_count = filters.shape[0]
    seq_rows = filters.shape[1]
    devices = lax.axis_size("seq")
    shard_index = lax.axis_index("seq")
    seq_length = seq_rows * devices
    grad_scale = 1.0 / math.sqrt(seq_length)
    all_inputs = lax.all_gather(inputs, "chan", axis=0, tiled=True)
    projected = jnp.einsum("cd,ct->dt", value_weight, all_inputs, precision=HIGHEST)
    query_proj = jnp.einsum("cd,ct->dt", query_weight, all_inputs, precision=HIGHEST)
    gated_grad = grad_out * query_proj
    signals = jnp.stack([projected, filters, gated_grad])
    position = shard_index * seq_rows + jnp.arange(seq_rows, dtype=jnp.int32)
    twist_angle = 0.5 * math.pi / seq_length * position.astype(jnp.float32)
    cosine = jnp.cos(twist_angle)
    sine_part = jnp.sin(twist_angle)
    twisted = jnp.stack([signals * cosine, -signals * sine_part])
    columns = jnp.transpose(twisted, (0, 3, 1, 2)).reshape(2, seq_rows, 3 * channel_count)
    spectra = forward(columns, shard_index, devices, BLK).reshape(2, seq_rows, 3, channel_count)
    value_spec = spectra[:, :, 0]
    filter_spec = spectra[:, :, 1]
    grad_spec = spectra[:, :, 2]
    products = jnp.stack(
        [
            multiply(filter_spec, value_spec, False),
            multiply(filter_spec, grad_spec, True),
            multiply(value_spec, grad_spec, True),
        ],
        axis=2,
    )
    restored = inverse(
        products.reshape(2, seq_rows, 3 * channel_count), shard_index, devices, BLK
    ).reshape(2, seq_rows, 3, channel_count)
    combined = restored[0] * cosine[:, None, None] - restored[1] * sine_part[:, None, None]
    combined = jnp.transpose(combined, (1, 2, 0))
    convolved = combined[0]
    grad_value = combined[1]
    filter_grad = combined[2] * grad_scale
    grad_query = grad_out * convolved
    input_grad = lax.psum_scatter(
        jnp.dot(value_weight, grad_value, precision=HIGHEST, preferred_element_type=jnp.float32)
        + jnp.dot(query_weight, grad_query, precision=HIGHEST, preferred_element_type=jnp.float32),
        "chan",
        scatter_dimension=0,
        tiled=True,
    )
    partial_value = jnp.einsum("ct,dt->cd", all_inputs, grad_value, precision=HIGHEST) * grad_scale
    partial_query = jnp.einsum("ct,dt->cd", all_inputs, grad_query, precision=HIGHEST) * grad_scale
    value_gradient, query_gradient = lax.psum((partial_value, partial_query), "seq")
    return (input_grad, filter_grad, value_gradient, query_gradient)


NN = (((1,), (0,)), ((), ()))
NT = (((1,), (1,)), ((), ()))
scope = jax.named_scope


def split_table(table):
    high = table.astype(jnp.bfloat16)
    low = (table - high.astype(np.float32)).astype(jnp.bfloat16)
    return high, low


@functools.lru_cache(maxsize=None)
def transform_tables(seq_length):
    outer = seq_length // LANES
    k = np.arange(outer, dtype=np.float64)
    a = np.arange(outer, dtype=np.float64)
    b = np.arange(LANES, dtype=np.float64)
    phase = 2 * np.pi * np.outer(4 * k + 1, a) % (2 * np.pi * 4 * outer) / (4 * outer)
    small = np.concatenate([np.cos(phase), -np.sin(phase)], axis=0)
    wide_h, wide_l = split_table(small.astype(np.float32))
    tall_h, tall_l = split_table((small.T / seq_length).astype(np.float32))
    angle = 2 * np.pi * np.outer(4 * k + 1, b) / (4 * seq_length)
    turn = np.stack([np.cos(angle), np.sin(angle)]).astype(np.float32)
    inner = 2 * np.pi * (np.outer(b, b) % LANES) / LANES
    c, s = np.cos(inner), np.sin(inner)
    ahead_h, ahead_l = split_table(np.block([[c, -s], [s, c]]).astype(np.float32))
    back_h, back_l = split_table(np.block([[c, s], [-s, c]]).astype(np.float32))
    first = slice(0, outer // 2)
    return (
        np.concatenate([wide_h, wide_l, wide_h, wide_l], axis=1),
        np.concatenate([tall_h, tall_l, tall_h, tall_l], axis=1),
        np.concatenate([t[:, first] for t in (wide_h, wide_l, wide_h, wide_l)], axis=1),
        np.concatenate([t[first] for t in (tall_h, tall_l, tall_h, tall_l)], axis=1),
        np.concatenate([ahead_h, ahead_h, ahead_l], axis=0),
        np.concatenate([back_h, back_h, back_l], axis=0),
        turn,
    )


def split(x):
    high = x.astype(jnp.bfloat16)
    return high, (x - high.astype(jnp.float32)).astype(jnp.bfloat16)


def dot3(first, second, dims=NN):
    def dot(x, y):
        return lax.dot_general(x, y, dims, preferred_element_type=jnp.float32)

    return dot(first[0], second[0]) + (dot(first[0], second[1]) + dot(first[1], second[0]))


def dot(first, second):
    return lax.dot_general(first, second, NN, preferred_element_type=jnp.float32)


def left3(x):
    high, low = split(x)
    return jnp.concatenate([high, low, high], axis=1)


def right4(x):
    high, low = split(x)
    return jnp.concatenate([high, high, low, low], axis=0)


def fused_kernel(devices, scale, *refs):
    x_hbm, vw_hbm, qw_hbm, f_hbm, g_hbm = refs[:5]
    table_hbm = refs[5:12]
    ig_out, fg_out, vg_out, qg_out = refs[12:16]
    x_ref, vw_ref, qw_ref, g_ref = refs[16:20]
    table_refs = refs[20:27]
    wide_ref, tall_ref, wide_loc_ref, tall_loc_ref, ahead_ref, back_ref, turn_ref = table_refs
    other_x, f_sig, send_sig, in_sig, spec, out_sig, ret_sig, part, scat, red, gath = refs[27:38]
    loc_sig, loc_spec, loc_out, loc_ret, ig_send, ig_recv = refs[38:44]
    ssem, rsem, csend, crecv, lsem = refs[44:]
    me = lax.axis_index("seq")
    chan = lax.axis_index("chan")
    half, width = x_ref.shape
    pieces = width // LANES
    inner = devices // 2
    outer = devices // inner
    rows = 2 * half // inner
    me_inner, me_outer = me % inner, me // inner
    near = devices // 2
    low = me < near
    high = me >= near

    steps = []
    while 1 << len(steps) < devices:
        bit = 1 << len(steps)
        steps.append((1 - 2 * (me // bit % 2)) * bit)

    def peer_of(i):
        return me + sum(step for at, step in enumerate(steps) if i >> at & 1)

    barrier = pltpu.get_barrier_semaphore()

    for index in reversed(range(1, devices)):
        pl.semaphore_signal(
            barrier,
            inc=1,
            device_id={"seq": peer_of(index)},
            device_id_type=pl.DeviceIdType.MESH,
        )
    pl.semaphore_signal(
        barrier, inc=1, device_id={"chan": 1 - chan}, device_id_type=pl.DeviceIdType.MESH
    )

    def lanes(piece):
        return slice(piece * LANES, (piece + 1) * LANES)

    loads = [
        pltpu.make_async_copy(src, dst, lsem.at[max(at - pieces + 1, 0)])
        for at, (src, dst) in enumerate(
            [
                *(
                    (f_hbm.at[:, :, lanes(piece)], f_sig.at[:, piece])
                    for piece in range(pieces)
                ),
                (x_hbm, x_ref),
                (vw_hbm, vw_ref),
                (qw_hbm, qw_ref),
                (g_hbm, g_ref),
                *zip(table_hbm, table_refs),
            ]
        )
    ]
    for load in loads:
        load.start()

    def wait_loads(count):
        for load in loads[:count]:
            load.wait()
        del loads[:count]

    @pl.when(high)
    def _():
        in_sig[2, : near * pieces] = jnp.zeros_like(in_sig[2, : near * pieces])

    pl.semaphore_wait(barrier, devices)

    def exchange(index, src, dst):
        return pltpu.make_async_remote_copy(
            src_ref=src,
            dst_ref=dst,
            send_sem=csend.at[index],
            recv_sem=crecv.at[index],
            device_id={"chan": 1 - chan},
            device_id_type=pl.DeviceIdType.MESH,
        )

    def send_each(slot, src_of, dst, count=devices, stride=1, first=1):
        for index in reversed(range(first, count)):
            peer = peer_of(index * stride)
            pltpu.make_async_remote_copy(
                src_ref=src_of(peer),
                dst_ref=dst,
                send_sem=ssem.at[slot],
                recv_sem=rsem.at[slot],
                device_id={"seq": peer},
                device_id_type=pl.DeviceIdType.MESH,
            ).start()

    def drain(slot, ref, what):
        copy = pltpu.make_async_remote_copy(
            src_ref=ref,
            dst_ref=ref,
            send_sem=ssem.at[slot],
            recv_sem=rsem.at[slot],
            device_id={"seq": peer_of(1)},
            device_id_type=pl.DeviceIdType.MESH,
        )
        getattr(copy, what)()

    def group_rows(peer, count):
        return pl.ds(pl.multiple_of(peer * count, count), count)

    def messages(slot, count, what):
        drain(slot, in_sig.at[0, pl.ds(0, count * pieces)], what)

    def split_messages(slot, few, what):
        @pl.when(few)
        def _():
            messages(slot, near - 1, what)

        @pl.when(jnp.logical_not(few))
        def _():
            messages(slot, devices - 1, what)

    def out_way(slot, what):
        src = f_sig if slot == 0 else send_sig.at[slot - 1]
        mine = in_sig.at[slot, group_rows(me, pieces)]
        if what == "start":
            if slot < 2:
                send_each(slot, lambda p: src.at[p], mine, devices, 1, near)
            else:

                @pl.when(high)
                def _():
                    send_each(slot, lambda p: src.at[p], mine, devices, 1, near)

            send_each(slot, lambda p: src.at[p], mine, near)
            in_sig[slot, group_rows(me, pieces)] = src[me]

            @pl.when(low)
            def _():
                own = group_rows(me, pieces)
                send_each(12 + slot, lambda p: src.at[p + near], loc_sig.at[slot, own], near)
                loc_sig[slot, own] = src[me + near]

        elif slot < 2:
            messages(slot, devices - 1, what)
        else:
            split_messages(slot, high if what == "wait_recv" else low, what)

    def back_way(slot, what):
        def send(count, first):
            send_each(
                3 + slot,
                lambda p: out_sig.at[slot, group_rows(p, pieces)],
                ret_sig.at[slot, me],
                count,
                1,
                first,
            )

        if what == "start":
            if slot > 0:
                send(devices, near)
            else:

                @pl.when(low)
                def _():
                    send(devices, near)

            send(near, 1)
            ret_sig[slot, me] = out_sig[slot, group_rows(me, pieces)]
        elif slot > 0:
            messages(3 + slot, devices - 1, what)
        else:
            split_messages(3, low if what == "wait_recv" else high, what)

    def back_local(slot):
        own = ret_sig.at[0, me + near] if slot == 0 else loc_ret.at[slot - 1, me]
        send_each(
            15 + slot, lambda p: loc_out.at[slot, group_rows(p, pieces)], own, near
        )
        own[...] = loc_out[slot, group_rows(me, pieces)]

    def scatter(slot, what):
        if what == "start":
            send_each(
                6 + slot,
                lambda p: part.at[slot, group_rows(p % inner, rows), :],
                scat.at[slot, me_inner],
                inner,
            )
        else:
            drain(6 + slot, scat.at[slot, pl.ds(0, inner - 1)], what)

    def swap(slot, what):
        if what == "start":
            send_each(
                8 + slot,
                lambda p: red.at[slot, me_outer],
                red.at[slot, me_outer],
                outer,
                inner,
            )
        else:
            drain(8 + slot, red.at[slot, pl.ds(0, outer - 1)], what)

    def gather(slot, what):
        mine = gath.at[slot, group_rows(me_inner, rows), :]
        if what == "start":
            send_each(10 + slot, lambda p: mine, mine, inner)
        else:
            drain(10 + slot, gath.at[slot, pl.ds(0, (inner - 1) * rows), :], what)

    give_x = exchange(0, x_hbm, other_x)
    give_x.start()
    with scope("load_f"):
        pltpu.make_async_copy(f_sig, f_sig, lsem.at[0]).wait()
        del loads[:pieces]
    with scope("out0"):
        out_way(0, "start")

    wait_loads(3)
    own_rows = pl.ds(pl.multiple_of(chan * half, half), half)
    other_rows = pl.ds(pl.multiple_of((1 - chan) * half, half), half)
    own_x = split(x_ref[...])
    partial_value = dot3(split(vw_ref[own_rows, :].T), own_x)
    partial_query = dot3(split(qw_ref[own_rows, :].T), own_x)
    with scope("give_x"):
        give_x.wait()

    def stage(slot, value):
        for piece in range(pieces):
            send_sig[slot - 1, :, piece] = value[:, lanes(piece)].reshape(devices, GROUP, LANES)
        with scope("out"):
            out_way(slot, "start")

    far_x = split(other_x[...])
    stage(1, partial_value + dot3(split(vw_ref[other_rows, :].T), far_x))
    query_proj = partial_query + dot3(split(qw_ref[other_rows, :].T), far_x)
    wait_loads(1)
    stage(2, g_ref[...] * query_proj)

    wait_loads(len(loads))
    wide = wide_ref[...]
    tall = tall_ref[...]
    ahead = ahead_ref[...]
    back = back_ref[...]
    cosine = turn_ref[0]
    sine = turn_ref[1]
    outer_len = cosine.shape[0]

    def channel_rows(channel):
        return slice(channel * outer_len, (channel + 1) * outer_len)

    def transform(source, table, target):
        count = source.shape[0]
        signal = source.reshape(count * GROUP, LANES)
        rows_of = []
        for pair in range(0, GROUP, 2):
            columns = jnp.concatenate(
                [
                    signal[pl.ds(channel, count, stride=GROUP), :]
                    for channel in (pair, pair + 1)
                ],
                axis=1,
            )
            first = dot(table, right4(columns))
            for at in range(2):
                real = first[:outer_len, lanes(at)]
                imag = first[outer_len:, lanes(at)]
                rows_of.append(
                    jnp.concatenate(
                        [real * cosine + imag * sine, imag * cosine - real * sine], axis=1
                    )
                )
        target[...] = dot(left3(jnp.concatenate(rows_of, axis=0)), ahead)

    def restore(first, second, conjugate, table, target, factor=None):
        count = target.shape[0]
        real_a, imag_a = first[:, :LANES], first[:, LANES:]
        real_b, imag_b = second[:, :LANES], second[:, LANES:]
        if conjugate:
            imag_a = -imag_a
        product = jnp.concatenate(
            [real_a * real_b - imag_a * imag_b, real_a * imag_b + imag_a * real_b], axis=1
        )
        inverse = dot(left3(product), back)
        result = target.reshape(count * GROUP, LANES)
        for pair in range(0, GROUP, 2):
            columns = []
            for channel in (pair, pair + 1):
                real = inverse[channel_rows(channel), :LANES]
                imag = inverse[channel_rows(channel), LANES:]
                columns.append(
                    jnp.concatenate(
                        [real * cosine - imag * sine, imag * cosine + real * sine], axis=0
                    )
                )
            signal = dot(table, right4(jnp.concatenate(columns, axis=1)))
            if factor is not None:
                signal = signal * factor
            for at in range(2):
                result[pl.ds(pair + at, count, stride=GROUP), :] = signal[:, lanes(at)]

    def returned(slot):
        return jnp.concatenate(
            [ret_sig[slot, :, piece].reshape(half, LANES) for piece in range(pieces)], axis=1
        )

    def local_transform(slot):
        with scope(f"locw{slot}"):
            messages(12 + slot, near - 1, "wait_recv")
        transform(loc_sig.at[slot], wide_loc_ref[...], loc_spec.at[slot])

    def local_restore(first, second, conjugate, slot, factor=None):
        restore(
            loc_spec.at[first],
            loc_spec.at[second],
            conjugate,
            tall_loc_ref[...],
            loc_out.at[slot],
            factor,
        )

    with scope("wait0"):
        out_way(0, "wait_recv")
    with scope("t0"):
        transform(in_sig.at[0], wide, spec.at[0])
    @pl.when(low)
    def _():
        local_transform(0)
        local_transform(1)
        with scope("locr0"):
            local_restore(0, 1, False, 0)
        back_local(0)

    with scope("wait1"):
        out_way(1, "wait_recv")
    with scope("t1"):
        transform(in_sig.at[1], wide, spec.at[1])
    with scope("r0"):
        restore(spec.at[0], spec.at[1], False, tall, out_sig.at[0])
        back_way(0, "start")

    @pl.when(low)
    def _():
        local_transform(2)
        with scope("locr1"):
            local_restore(0, 2, True, 1)
        back_local(1)
        with scope("locr2"):
            local_restore(1, 2, True, 2, scale)

    with scope("wait2"):
        out_way(2, "wait_recv")
    with scope("t2"):
        transform(in_sig.at[2], wide, spec.at[2])
    with scope("r1"):
        restore(spec.at[0], spec.at[2], True, tall, out_sig.at[1])
        back_way(1, "start")

    with scope("r2"):
        restore(spec.at[1], spec.at[2], True, tall, out_sig.at[2], scale)

    def back_ready(slot):
        with scope(f"back{slot}"):
            back_way(slot, "wait_recv")

            @pl.when(low)
            def _():
                messages(15 + slot, near - 1, "wait_recv")
                if slot > 0:
                    ret_sig[slot, near:] = ret_sig[slot, near:] + loc_ret[slot - 1]

    def weight_part(slot, grad):
        part[slot, own_rows, :] = dot3(own_x2, grad, NT)
        part[slot, other_rows, :] = dot3(far_x2, grad, NT)
        scatter(slot, "start")
        scat[slot, me_inner] = part[slot, group_rows(me_inner, rows), :]

    own_x2 = split(x_ref[...])
    far_x2 = split(other_x[...])
    back_ready(0)
    grad_query = split(g_ref[...] * returned(0))
    weight_part(0, grad_query)

    @pl.when(high)
    def _():
        back_way(2, "start")

    near_grad = dot3(split(qw_ref[own_rows, :]), grad_query)
    far_grad = dot3(split(qw_ref[other_rows, :]), grad_query)

    def reduce_inner(slot):
        with scope(f"scat{slot}"):
            scatter(slot, "wait_recv")
        total = scat[slot, 0]
        for source in range(1, inner):
            total = total + scat[slot, source]
        red[slot, me_outer] = total
        swap(slot, "start")

    def reduce_outer(slot):
        with scope(f"swap{slot}"):
            swap(slot, "wait_recv")
        total = red[slot, 0]
        for source in range(1, outer):
            total = total + red[slot, source]
        gath[slot, group_rows(me_inner, rows), :] = total * scale
        gather(slot, "start")

    back_ready(1)
    grad_value = split(returned(1))
    weight_part(1, grad_value)
    ig_send[...] = far_grad + dot3(split(vw_ref[other_rows, :]), grad_value)
    give_ig = exchange(1, ig_send, ig_recv)
    give_ig.start()
    reduce_inner(0)
    reduce_inner(1)

    @pl.when(low)
    def _():
        back_way(2, "start")
        back_local(2)

    near_grad = near_grad + dot3(split(vw_ref[own_rows, :]), grad_value)
    reduce_outer(0)
    with scope("give_ig"):
        give_ig.wait()
    ig_out[...] = near_grad + ig_recv[...]
    reduce_outer(1)
    back_ready(2)
    fg_out[...] = returned(2)
    for slot, out in ((0, qg_out), (1, vg_out)):
        with scope(f"gather{slot}"):
            gather(slot, "wait_recv")
        out[...] = gath[slot]
    with scope("sends"):
        for slot in range(3):
            out_way(slot, "wait_send")
            back_way(slot, "wait_send")
        for slot in range(2):
            scatter(slot, "wait_send")
            swap(slot, "wait_send")
            gather(slot, "wait_send")

        @pl.when(low)
        def _():
            for slot in range(12, 18):
                messages(slot, near - 1, "wait_send")


def finish_kernel(*refs):
    stores = [
        pltpu.make_async_copy(source, target, refs[8].at[at])
        for at, (source, target) in enumerate(zip(refs[:4], refs[4:8]))
    ]
    for store in stores:
        store.start()
    for store in stores:
        store.wait()


def fused_device(inputs, value_weight, query_weight, filters, grad_out):
    half, width = inputs.shape
    devices = lax.axis_size("seq")
    seq_length = width * devices
    depth = value_weight.shape[0]
    inner = devices // 2
    outer = devices // inner
    rows = depth // inner
    tables = transform_tables(seq_length)
    pieces = width // LANES
    outer_len = seq_length // LANES
    tables = [jnp.asarray(t) for t in tables]
    hbm = pl.BlockSpec(memory_space=pltpu.HBM)
    vmem = pl.BlockSpec(memory_space=pltpu.VMEM)
    f32 = jnp.float32
    outs = (
        jax.ShapeDtypeStruct((half, width), f32),
        jax.ShapeDtypeStruct((half, width), f32),
        jax.ShapeDtypeStruct((depth, half), f32),
        jax.ShapeDtypeStruct((depth, half), f32),
    )
    results = pl.pallas_call(
        functools.partial(fused_kernel, devices, 1.0 / math.sqrt(seq_length)),
        out_shape=tuple(pltpu.VMEM(out.shape, out.dtype) for out in outs),
        in_specs=[hbm] * (5 + len(tables)),
        out_specs=(vmem,) * 4,
        scratch_shapes=[
            pltpu.VMEM((half, width), f32),
            pltpu.VMEM((depth, half), f32),
            pltpu.VMEM((depth, half), f32),
            pltpu.VMEM((half, width), f32),
            *(pltpu.VMEM(t.shape, t.dtype) for t in tables),
            pltpu.VMEM((half, width), f32),
            pltpu.VMEM((devices, pieces, GROUP, LANES), f32),
            pltpu.VMEM((2, devices, pieces, GROUP, LANES), f32),
            pltpu.VMEM((3, outer_len, GROUP, LANES), f32),
            pltpu.VMEM((3, outer_len * GROUP, 2 * LANES), f32),
            pltpu.VMEM((3, outer_len, GROUP, LANES), f32),
            pltpu.VMEM((3, devices, pieces, GROUP, LANES), f32),
            pltpu.VMEM((2, depth, half), f32),
            pltpu.VMEM((2, inner, rows, half), f32),
            pltpu.VMEM((2, outer, rows, half), f32),
            pltpu.VMEM((2, depth, half), f32),
            pltpu.VMEM((3, outer_len // 2, GROUP, LANES), f32),
            pltpu.VMEM((3, outer_len * GROUP, 2 * LANES), f32),
            pltpu.VMEM((3, outer_len // 2, GROUP, LANES), f32),
            pltpu.VMEM((2, devices // 2, pieces, GROUP, LANES), f32),
            pltpu.VMEM((half, width), f32),
            pltpu.VMEM((half, width), f32),
            pltpu.SemaphoreType.DMA((18,)),
            pltpu.SemaphoreType.DMA((18,)),
            pltpu.SemaphoreType.DMA((2,)),
            pltpu.SemaphoreType.DMA((2,)),
            pltpu.SemaphoreType.DMA((5 + len(tables),)),
        ],
        compiler_params=pltpu.CompilerParams(
            collective_id=0, has_side_effects=True, vmem_limit_bytes=60 * 1024 * 1024
        ),
    )(
        inputs,
        value_weight,
        query_weight,
        filters.reshape(devices, GROUP, width),
        grad_out,
        *tables,
    )
    return tuple(
        pl.pallas_call(
            finish_kernel,
            out_shape=outs,
            in_specs=[vmem] * 4,
            out_specs=(hbm,) * 4,
            scratch_shapes=[pltpu.SemaphoreType.DMA((4,))],
        )(*(pltpu.with_memory_space_constraint(r, pltpu.VMEM) for r in results))
    )


def on_device(inputs, value_weight, query_weight, filters, grad_out):
    channel_count, width = filters.shape
    devices = lax.axis_size("seq")
    fits = (
        channel_count == GROUP * devices
        and channel_count == inputs.shape[0]
        and lax.axis_size("chan") == 2
        and width % LANES == 0
        and channel_count % LANES == 0
        and devices & (devices - 1) == 0
        and (width * devices // LANES) % 32 == 0
        and value_weight.shape[0] % (GROUP * devices) == 0
    )
    body = fused_device if fits else per_device
    return body(inputs, value_weight, query_weight, filters, grad_out)


def solution(mesh):
    return jax.shard_map(
        on_device,
        mesh=mesh,
        in_specs=(
            P("chan", "seq"),
            P(None, "chan"),
            P(None, "chan"),
            P("chan", "seq"),
            P("chan", "seq"),
        ),
        out_specs=(P("chan", "seq"), P("chan", "seq"), P(None, "chan"), P(None, "chan")),
        check_vma=False,
    )
```
